32 devices in a mesh: grp: 2 (over x), row: 16 (over z, y, core).
Axes of the slice: x: 2, y: 2, z: 4, core: 2. Of those that a mesh axis runs over, the one named last changes fastest.
Arguments:
- aligned_sequences: bfloat16 [32, 64, 64], P(None, ('grp', 'row')), parts along dimension 1, may hold values from -6 to 6
- first_factor_matrix: bfloat16 [64, 32], replicated, may hold values from -0.75 to 0.75
- second_factor_matrix: bfloat16 [64, 32], replicated, may hold values from -0.75 to 0.75
- tensor_matrix: bfloat16 [1024, 128], replicated, may hold values from -1 to 1
- tensor_offset: bfloat16 [128], replicated, may hold values from -4 to 4
- structural_duplex_patches: bfloat16 [512, 2048], P(('grp', 'row')), parts along dimension 0, may hold values from -6 to 6
- patch_source_index: int32 [512, 1], P(('grp', 'row')), parts along dimension 0, may hold values from 0 to 15; in each aligned block of 16 rows (0 to 15, 16 to 31, ...) at most 2 rows name the same one
- patch_target_index: int32 [512], P(('grp', 'row')), parts along dimension 0, may hold values from 0 to 1
- structural_matrix: bfloat16 [64, 128], replicated, may hold values from -0.75 to 0.75
- polymer_residue_lengths: int32 [16], P('grp'), parts along dimension 0, may hold values from 1 to 16, 32 in all
- sigmoid_matrix: bfloat16 [128, 128], replicated, may hold values from -0.5 to 0.5
- content_matrix: bfloat16 [128, 128], replicated, may hold values from -0.5 to 0.5
Outputs:
- update: bfloat16 [64, 32, 128], P(('grp', 'row')), parts along dimension 0
The draws below stay inside these ranges and needn't reach their ends.
There are 2 independent parts, one for each index of `grp`. The reference program is written for one: setup_inputs(seed, part) draws one part's arguments, and reference() takes and returns one part's arrays. A program takes and returns all parts, laid end to end along the dimension named above; an argument that names none is the same for every part. Nothing has to cross between parts.
Inputs may be any that keep to these rules, and one draw needn't show every extreme that they name: `patch_source_index`: among the tiles of one device no owner is named more than 2 times, a bound that some block reaches.
All inputs are finite; a program needn't handle non-finite values.
Results may differ from the reference program's by a relative error of at most 0.0073.
Values may be sent and summed in bfloat16 or wider, within the bound.
No kernel may reach another device: no remote copies, remote signals or barrier semaphores. Data moves between devices by JAX's collectives and lax.ppermute only.
A program may use at most 64 MiB of HBM per device.

```python
import math
import jax
import jax.numpy as jnp
import numpy as np
from jax import lax

ALIGNED_FEATURES = 64
FACTOR_FEATURES = 32
DUPLEX_FEATURES = 128
C_T = 64
ALIGNED_DEPTH = 32
TOK_DEV = 2
TC = 16
CAP = 2
CHAINS = 8
RESIDUE_TOTAL = 32
CT = 2
SLOTS = 16
N_ROW = 16


def plant(drawn, key, low, top_value):
    spot = [jax.random.randint(jax.random.fold_in(key, axis), (), 0, length) for axis, length in enumerate(drawn.shape)]
    widest = drawn.shape.index(max(drawn.shape))
    next_to = spot[:widest] + [(spot[widest] + 1) % drawn.shape[widest]] + spot[widest + 1:]
    return drawn.at[tuple(spot)].set(low).at[tuple(next_to)].set(top_value)


def levels(stream_key, shape, cuts, smallest, top_value):
    loudness, own = 1.0, jax.random.fold_in(stream_key, 6)
    for position, blocks in cuts:
        heights = jnp.exp(jax.random.uniform(jax.random.fold_in(own, position), (blocks,), jnp.float32, smallest / len(cuts), top_value / len(cuts)))
        loudness = loudness * jnp.repeat(heights, shape[position] // blocks).reshape([-1 if axis == position else 1 for axis in range(len(shape))])
    return loudness


def split_up(number_of, total, reach, slope):
    weights = [(1 << 20) // math.isqrt(rank ** slope) + 1 for rank in range(2, number_of + 1)]
    rest, counts = total - reach - (number_of - 1), [1] * (number_of - 1)
    while rest > 0:
        candidates = [i for i in range(number_of - 1) if counts[i] < reach]
        pool, remaining = sum([weights[i] for i in candidates]), rest
        for i in candidates:
            more = min(reach - counts[i], max(1, remaining * weights[i] // pool), rest)
            counts[i] = counts[i] + more
            rest = rest - more
    return np.array([reach] + counts)


def uneven_parts(key, count, total, reach, slope):
    if count == 2:
        one = jax.random.randint(key, (), max(1, total - reach), min(reach, total - 1) + 1)
        return jnp.stack([one, total - one])
    sizes = jnp.asarray(split_up(count, total, reach, slope), jnp.int32)
    couples = (count - 1) // 2
    giver, taker = sizes[1:1 + 2 * couples:2], sizes[2:2 + 2 * couples:2]
    slack = jnp.minimum(giver - 1, reach - taker)
    passed = jax.random.randint(jax.random.fold_in(key, 1), (couples,), 0, 1 << 20) % (slack + 1)
    sizes = sizes.at[1:1 + 2 * couples:2].set(giver - passed).at[2:2 + 2 * couples:2].set(taker + passed)
    return sizes[jax.random.permutation(jax.random.fold_in(key, 2), count)]


def assign_block(own_key, own, number, rows, amount, top, reach, lean):
    ranking = jax.random.permutation(own_key, amount)
    crowded, ordinary = portions_of(amount, rows * top, reach, lean, True), portions_of(amount, rows * top, reach, lean, False)
    places = jnp.arange(amount)

    def named(lengths, offset_by):
        used = int((lengths > 0).sum())
        fixed = max(1, used // 4)
        shifted = fixed + (places - fixed + offset_by * (used - fixed)) % max(1, amount - fixed)
        return jnp.zeros((amount,), jnp.int32).at[ranking[jnp.where(places < fixed, places, shifted)]].set(jnp.asarray(lengths, jnp.int32))

    lengths = jnp.where(number % 4 == 0, named(crowded, number // 4), named(ordinary, number - number // 4 - 1))
    mixed = jax.random.permutation(jax.random.fold_in(own, 3), amount)
    donor, taker = mixed[0:amount // 2 * 2:2], mixed[1:amount // 2 * 2:2]
    margin = jnp.minimum(lengths[donor] - 1, reach - lengths[taker]) // 2
    margin = jnp.where((donor == ranking[0]) | (taker == ranking[0]) | (lengths[taker] == 0), 0, jnp.maximum(margin, 0))
    shifted = jax.random.randint(jax.random.fold_in(own, 4), (amount // 2,), 0, 1 << 20) % (margin + 1)
    lengths = lengths.at[donor].add(-shifted).at[taker].add(shifted)
    items = jnp.searchsorted(jnp.cumsum(lengths), jnp.arange(rows * top), side="right").astype(jnp.int32)
    listing = items.reshape(top, rows).T
    listing = listing[jax.random.permutation(jax.random.fold_in(own, 1), rows)]
    offset_by = jax.random.randint(jax.random.fold_in(own, 2), (rows, 1), 0, top)
    return jnp.take_along_axis(listing, (jnp.arange(top)[None, :] + offset_by) % top, axis=1)


def portions_of(amount, total, most, skew, full):
    portions = [(1 << 20) // math.isqrt(rank ** skew) + 1 for rank in range(1, amount + 1)]
    largest = most if full else min(most, max(-(-total // amount), total * portions[0] // sum(portions)))
    least = 1 if total - largest >= amount - 1 else 0
    counts, surplus = [largest] + [least] * (amount - 1), total - largest - least * (amount - 1)
    while surplus > 0:
        free = [i for i in range(1, amount) if counts[i] < largest] or [i for i in range(1, amount) if counts[i] < most]
        pool, remaining = sum([portions[i] for i in free]), surplus
        for i in free:
            addition = min(most - counts[i], max(1, remaining * portions[i] // pool), surplus)
            counts[i] = counts[i] + addition
            surplus = surplus - addition
    return np.array(counts)


def gaussian(own_key, dims, scale, limit, pieces=(), held_as=jnp.bfloat16):
    array = jax.random.normal(own_key, dims, jnp.float32) * scale
    if len(pieces) > 0:
        array = levels(own_key, dims, pieces, -0.22, 0.18) * array
    return jnp.clip(array, min=-limit, max=limit).astype(held_as)


def setup_inputs(seed: int = 0, part: int = 0) -> dict:
    seeds = jax.random.split(jax.random.key(seed), 13)
    part_keys = jax.random.split(jax.random.fold_in(seeds[12], part), 13)
    aligned_sequences = gaussian(part_keys[0], (ALIGNED_DEPTH, RESIDUE_TOTAL, ALIGNED_FEATURES), 1.0, 6.0, ((1, 16),))
    first_factor_matrix = gaussian(seeds[1], (ALIGNED_FEATURES, FACTOR_FEATURES), ALIGNED_FEATURES ** -0.5, 0.75)
    second_factor_matrix = gaussian(seeds[2], (ALIGNED_FEATURES, FACTOR_FEATURES), ALIGNED_FEATURES ** -0.5, 0.75)
    tensor_matrix = gaussian(seeds[3], (FACTOR_FEATURES * FACTOR_FEATURES, DUPLEX_FEATURES), (FACTOR_FEATURES * FACTOR_FEATURES // ALIGNED_DEPTH) ** -0.5, 1.0)
    tensor_offset = gaussian(seeds[4], (DUPLEX_FEATURES,), 1.0, 4.0)
    structural_duplex_patches = gaussian(part_keys[5], (N_ROW * SLOTS, TOK_DEV * TC * C_T), 1.0, 6.0, ((0, 16),))
    patch_source_index_keys = jax.random.split(jax.random.fold_in(part_keys[6], 1), (N_ROW * SLOTS) // SLOTS)
    patch_source_index_turns = jax.random.permutation(jax.random.fold_in(part_keys[6], 3), (N_ROW * SLOTS) // SLOTS)
    patch_source_index = jax.vmap(lambda own, number: assign_block(jax.random.fold_in(part_keys[6], 2), own, number, SLOTS, N_ROW, 1, CAP, 2))(patch_source_index_keys, patch_source_index_turns).reshape((N_ROW * SLOTS, 1))
    patch_target_index = plant(jax.random.randint(part_keys[7], (N_ROW * SLOTS,), 0, CT), jax.random.fold_in(part_keys[7], 1), 0, CT - 1).astype(jnp.int32)
    structural_matrix = gaussian(seeds[8], (C_T, DUPLEX_FEATURES), C_T ** -0.5, 0.75)
    polymer_residue_lengths = uneven_parts(part_keys[9], CHAINS, RESIDUE_TOTAL, RESIDUE_TOTAL // 2, 2).astype(jnp.int32)
    sigmoid_matrix = gaussian(seeds[10], (DUPLEX_FEATURES, DUPLEX_FEATURES), DUPLEX_FEATURES ** -0.5, 0.5)
    content_matrix = gaussian(seeds[11], (DUPLEX_FEATURES, DUPLEX_FEATURES), DUPLEX_FEATURES ** -0.5, 0.5)
    return dict(aligned_sequences=aligned_sequences, first_factor_matrix=first_factor_matrix, second_factor_matrix=second_factor_matrix, tensor_matrix=tensor_matrix, tensor_offset=tensor_offset, structural_duplex_patches=structural_duplex_patches, patch_source_index=patch_source_index, patch_target_index=patch_target_index, structural_matrix=structural_matrix, polymer_residue_lengths=polymer_residue_lengths, sigmoid_matrix=sigmoid_matrix, content_matrix=content_matrix)


def standardize_features(inputs):
    centred = inputs - lax.optimization_barrier(jnp.mean(inputs, axis=-1, keepdims=True))
    variance = lax.optimization_barrier(jnp.mean(centred * centred, axis=-1, keepdims=True))
    return centred * lax.rsqrt(variance + 1e-05)

def reference(aligned_sequences, first_factor_matrix, second_factor_matrix, tensor_matrix, tensor_offset, structural_duplex_patches, patch_source_index, patch_target_index, structural_matrix, polymer_residue_lengths, sigmoid_matrix, content_matrix):
    standardized_features = standardize_features(aligned_sequences.astype(jnp.float32)).astype(jnp.bfloat16)
    left_side = jnp.einsum('fvk,ko->fvo', standardized_features.astype(jnp.float32), first_factor_matrix.astype(jnp.float32)).astype(jnp.bfloat16)
    second_factor = jnp.einsum('fvk,ko->fvo', standardized_features.astype(jnp.float32), second_factor_matrix.astype(jnp.float32)).astype(jnp.bfloat16)
    target_ids = (patch_source_index[:, 0] * CT + patch_target_index).astype(jnp.int32)
    tile_sum = jax.ops.segment_sum(structural_duplex_patches.astype(jnp.float32), target_ids, num_segments=N_ROW * CT)
    tile_count = jax.ops.segment_sum(jnp.ones(target_ids.shape, jnp.float32), target_ids, num_segments=N_ROW * CT)
    tile_mean = tile_sum / jnp.maximum(tile_count, 1.0)[:, None]
    chain_ends = jnp.cumsum(polymer_residue_lengths)
    positions = jnp.arange(RESIDUE_TOTAL, dtype=jnp.int32)
    chain_of = lax.optimization_barrier(jnp.sum((positions[:, None] >= chain_ends[None, :]).astype(jnp.int32), axis=1))

    def one_block(owner_idx):
        offset = (owner_idx * TOK_DEV).astype(jnp.int32)
        block_tiles = lax.dynamic_slice_in_dim(tile_mean, (owner_idx * CT).astype(jnp.int32), CT, 0)
        block_tiles = block_tiles.reshape(CT, TOK_DEV, TC, C_T).transpose(1, 0, 2, 3).reshape(TOK_DEV, RESIDUE_TOTAL, C_T)
        row_chain = lax.dynamic_slice_in_dim(chain_of, offset, TOK_DEV)
        same_chain = (row_chain[:, None] == chain_of[None, :]).astype(jnp.float32)
        template_in = (block_tiles * same_chain[:, :, None]).astype(jnp.bfloat16)
        template_pair = jnp.einsum('ijc,cz->ijz', template_in.astype(jnp.float32), structural_matrix.astype(jnp.float32))
        first_factor_lines = lax.dynamic_slice_in_dim(left_side, offset, TOK_DEV, 1)
        tensor_contraction = jnp.einsum('iso,ift->sfot', first_factor_lines.astype(jnp.float32), second_factor.astype(jnp.float32)) / ALIGNED_DEPTH
        tensor_contraction = tensor_contraction.astype(jnp.bfloat16).reshape(TOK_DEV, RESIDUE_TOTAL, FACTOR_FEATURES * FACTOR_FEATURES)
        opm = jnp.einsum('ijk,kz->ijz', tensor_contraction.astype(jnp.float32), tensor_matrix.astype(jnp.float32)) + tensor_offset.astype(jnp.float32)
        pair = template_pair + opm
        pair_normed = standardize_features(pair).astype(jnp.bfloat16).astype(jnp.float32)
        gating = jax.nn.sigmoid(jnp.einsum('ijc,cz->ijz', pair_normed, sigmoid_matrix.astype(jnp.float32)))
        linear = jnp.einsum('ijc,cz->ijz', pair_normed, content_matrix.astype(jnp.float32))
        return (gating * linear).astype(jnp.bfloat16)
    blocks = lax.map(one_block, jnp.arange(N_ROW, dtype=jnp.int32))
    return blocks.reshape(RESIDUE_TOTAL, RESIDUE_TOTAL, DUPLEX_FEATURES)
```

```python
import functools

import jax
import jax.numpy as jnp
from jax import lax
from jax.experimental import pallas as pl
from jax.experimental.pallas import tpu as pltpu
from jax.sharding import PartitionSpec as P

CAP = 2
LANES = 128
CODE_ROWS = 8
VMEM = pltpu.MemorySpace.VMEM
SMEM = pltpu.MemorySpace.SMEM


def dot(a, b):
    return jnp.dot(a, b, preferred_element_type=jnp.float32)


def dot_nt(a, b):
    return lax.dot_general(a, b, (((1,), (1,)), ((), ())), preferred_element_type=jnp.float32)


def standardize(x):
    centred = x - jnp.mean(x, axis=-1, keepdims=True)
    variance = jnp.mean(centred * centred, axis=-1, keepdims=True)
    return centred * lax.rsqrt(variance + 1e-05)


def pack_kernel(n_devices, rows, x_ref, second_ref, tiles_ref, owner_ref, column_ref, send_ref, normed_ref, wide):
    depth, lines, _ = x_ref.shape
    slots, width = tiles_ref.shape
    tile_rows = width // LANES
    n_chan = second_ref.shape[0]
    right_rows = n_chan * depth // LANES
    x = x_ref[...].astype(jnp.float32)
    for t in range(lines):
        normed = standardize(x[:, t, :]).astype(jnp.bfloat16)
        normed_ref[pl.ds(t * depth, depth), :] = normed
        right = dot_nt(second_ref[...], normed)
        groups = n_chan // right_rows
        packed = jnp.concatenate(
            [right[b * right_rows : (b + 1) * right_rows] for b in range(groups)], axis=1
        )
        for d in range(n_devices):
            wide[pl.ds(d * rows + t * right_rows, right_rows), :] = packed
    owner = owner_ref[...]
    here = lax.broadcasted_iota(jnp.int32, (slots, slots), 0)
    there = lax.broadcasted_iota(jnp.int32, (slots, slots), 1)
    across = jnp.broadcast_to(owner, (slots, slots))
    down = jnp.sum(jnp.where(here == there, across, 0), axis=1, keepdims=True)
    rank = jnp.sum(jnp.where((down == across) & (here < there), 1, 0), axis=0, keepdims=True)
    target = rank * n_devices + owner
    place = lax.broadcasted_iota(jnp.int32, (CAP * n_devices, slots), 0) == target
    base = lines * right_rows
    code = jnp.where(place, (column_ref[...] + 1).astype(jnp.float32), 0.0)
    code = jnp.sum(code, axis=1, keepdims=True)
    code = jnp.broadcast_to(code, (CAP * n_devices, LANES))
    place = place.astype(jnp.bfloat16)
    for q in range(tile_rows):
        placed = dot(place, tiles_ref[:, q * LANES : (q + 1) * LANES])
        for c in range(CAP):
            wide[pl.ds(base + c * tile_rows + q, n_devices, stride=rows), :] = placed[
                c * n_devices : (c + 1) * n_devices
            ]
    base = base + CAP * tile_rows
    for c in range(CODE_ROWS):
        piece = min(c, CAP - 1)
        wide[pl.ds(base + c, n_devices, stride=rows), :] = code[piece * n_devices : (piece + 1) * n_devices]
    send_ref[...] = wide[...].astype(jnp.bfloat16)


def left_kernel(
    n_tiles, tc, normed_ref, first_ref, tensor_ref, lengths_ref, device_ref, folded_ref, same_ref
):
    n_chan = first_ref.shape[0]
    pair_chan = tensor_ref.shape[2]
    lines = folded_ref.shape[1] // pair_chan
    depth = normed_ref.shape[0] // lines
    left = dot_nt(normed_ref[...], first_ref[...]).astype(jnp.bfloat16)
    right_rows = n_chan * depth // LANES
    groups = n_chan // right_rows
    for d in range(n_chan):
        part = (dot(left, tensor_ref[d]) / depth).astype(jnp.bfloat16)
        at = (d % right_rows) * LANES + (d // right_rows) * depth
        for t in range(lines):
            folded_ref[pl.ds(at, depth), t * pair_chan : (t + 1) * pair_chan] = part[
                t * depth : (t + 1) * depth
            ]
    height, _ = same_ref.shape
    tile_rows = height // n_tiles
    per_row = tile_rows // lines
    packed = tc // per_row
    row = lax.broadcasted_iota(jnp.int32, same_ref.shape, 0)
    lane = lax.broadcasted_iota(jnp.int32, same_ref.shape, 1)
    column = (row // tile_rows) * tc + (row % per_row) * packed + lane // (LANES // packed)
    line = device_ref[0] * lines + (row % tile_rows) // per_row
    end = jnp.int32(0)
    column_chain = jnp.zeros_like(column)
    line_chain = jnp.zeros_like(line)
    for c in range(lengths_ref.shape[0]):
        end = end + lengths_ref[c]
        column_chain = column_chain + (column >= end).astype(jnp.int32)
        line_chain = line_chain + (line >= end).astype(jnp.int32)
    same_ref[...] = (column_chain == line_chain).astype(jnp.float32)


def pair_kernel(
    n_devices,
    rows,
    tc,
    got_ref,
    folded_ref,
    same_ref,
    offset_ref,
    structural_ref,
    sigmoid_ref,
    content_ref,
    out_ref,
    right_wide,
    sums,
    pair,
):
    n_temp, pair_chan = structural_ref.shape
    lines = folded_ref.shape[1] // pair_chan
    depth_chan = folded_ref.shape[0]
    right_rows = depth_chan // LANES
    n_tokens = n_devices * lines
    height = same_ref.shape[0]
    n_tiles = n_tokens // tc
    tile_rows = height // n_tiles
    base = lines * right_rows
    code_base = base + CAP * tile_rows

    sums[...] = jnp.zeros_like(sums)

    def add_source(d, carry):
        start = pl.multiple_of(d * rows, 8)
        right_wide[pl.ds(pl.multiple_of(d * base, 8), base), :] = got_ref[pl.ds(start, base), :].astype(
            jnp.float32
        )
        codes = got_ref[pl.ds(start + code_base, CODE_ROWS), :].astype(jnp.float32)
        counts = list(carry)
        for c in range(CAP):
            tile = got_ref[pl.ds(start + base + c * tile_rows, tile_rows), :].astype(jnp.float32)
            code = codes[c : c + 1, :]
            for k in range(n_tiles):
                hit = code == k + 1.0
                counts[k] = counts[k] + jnp.where(hit, 1.0, 0.0)
                at = pl.ds(k * tile_rows, tile_rows)
                sums[at, :] = sums[at, :] + jnp.where(hit, tile, 0.0)
        return tuple(counts)

    counts = tuple(jnp.zeros((1, LANES), jnp.float32) for _ in range(n_tiles))
    counts = lax.fori_loop(0, n_devices, add_source, counts, unroll=n_devices <= 16)
    for k in range(n_tiles):
        at = pl.ds(k * tile_rows, tile_rows)
        mean = sums[at, :] / jnp.maximum(counts[k], 1.0)
        template = (mean * same_ref[at, :]).astype(jnp.bfloat16)
        for h in range(LANES // n_temp):
            part = dot(template[:, h * n_temp : (h + 1) * n_temp], structural_ref[...])
            per_row = tile_rows // lines
            for t in range(lines):
                pair[pl.ds(t * n_tokens + k * tc + h, per_row, stride=LANES // n_temp), :] = part[
                    t * per_row : (t + 1) * per_row
                ]
    outer = None
    for g in range(right_rows):
        lhs = right_wide[pl.ds(g, n_tokens, stride=right_rows), :].astype(jnp.bfloat16)
        term = dot(lhs, folded_ref[pl.ds(g * LANES, LANES), :])
        outer = term if outer is None else outer + term
    for t in range(lines):
        at = pl.ds(t * n_tokens, n_tokens)
        total = pair[at, :] + (outer[:, t * pair_chan : (t + 1) * pair_chan] + offset_ref[...])
        pair_normed = standardize(total).astype(jnp.bfloat16)
        gate = jax.nn.sigmoid(dot(pair_normed, sigmoid_ref[...]))
        linear = dot(pair_normed, content_ref[...])
        out_ref[at, :] = (gate * linear).astype(out_ref.dtype)


def on_device(
    aligned_sequences,
    first_factor_matrix,
    second_factor_matrix,
    tensor_matrix,
    tensor_offset,
    structural_duplex_patches,
    patch_source_index,
    patch_target_index,
    structural_matrix,
    polymer_residue_lengths,
    sigmoid_matrix,
    content_matrix,
):
    n_devices = lax.axis_size("row")
    device_id = lax.axis_index("row")
    depth, lines, n_feat = aligned_sequences.shape
    slots, width = structural_duplex_patches.shape
    n_chan = first_factor_matrix.shape[1]
    n_temp, pair_chan = structural_matrix.shape
    tc = width // (lines * n_temp)
    n_tokens = lines * n_devices
    n_tiles = n_tokens // tc
    tile_rows = width // LANES
    right_rows = n_chan * depth // LANES
    rows = lines * right_rows + CAP * tile_rows + CODE_ROWS
    vmem = pl.BlockSpec(memory_space=VMEM)
    smem = pl.BlockSpec(memory_space=SMEM)

    send, normed = pl.pallas_call(
        functools.partial(pack_kernel, n_devices, rows),
        out_shape=(
            jax.ShapeDtypeStruct((n_devices * rows, LANES), jnp.bfloat16),
            jax.ShapeDtypeStruct((lines * depth, n_feat), jnp.bfloat16),
        ),
        in_specs=[vmem] * 5,
        out_specs=(vmem, vmem),
        scratch_shapes=[pltpu.VMEM((n_devices * rows, LANES), jnp.float32)],
    )(
        aligned_sequences,
        second_factor_matrix.T,
        structural_duplex_patches,
        patch_source_index.reshape(1, slots),
        patch_target_index.reshape(1, slots),
    )
    got = lax.all_to_all(
        send.reshape(n_devices, rows, LANES), "row", split_axis=0, concat_axis=0, tiled=True
    ).reshape(n_devices * rows, LANES)
    folded, same = pl.pallas_call(
        functools.partial(left_kernel, n_tiles, tc),
        out_shape=(
            jax.ShapeDtypeStruct((n_chan * depth, lines * pair_chan), jnp.bfloat16),
            jax.ShapeDtypeStruct((n_tiles * tile_rows, LANES), jnp.float32),
        ),
        in_specs=[vmem] * 3 + [smem] * 2,
        out_specs=(vmem, vmem),
    )(
        normed,
        first_factor_matrix.T,
        tensor_matrix.reshape(n_chan, n_chan, pair_chan).transpose(1, 0, 2),
        polymer_residue_lengths,
        device_id.reshape(1),
    )
    out = pl.pallas_call(
        functools.partial(pair_kernel, n_devices, rows, tc),
        out_shape=jax.ShapeDtypeStruct((lines * n_tokens, pair_chan), jnp.bfloat16),
        in_specs=[vmem] * 7,
        out_specs=vmem,
        scratch_shapes=[
            pltpu.VMEM((n_devices * lines * right_rows, LANES), jnp.float32),
            pltpu.VMEM((n_tiles * tile_rows, LANES), jnp.float32),
            pltpu.VMEM((lines * n_tokens, pair_chan), jnp.float32),
        ],
    )(
        got,
        folded,
        same,
        tensor_offset.astype(jnp.float32).reshape(1, pair_chan),
        structural_matrix,
        sigmoid_matrix,
        content_matrix,
    )
    return out.reshape(lines, n_tokens, pair_chan)


def solution(mesh):
    placed = (
        P(None, ("grp", "row"), None),
        P(),
        P(),
        P(),
        P(),
        P(("grp", "row"), None),
        P(("grp", "row"), None),
        P(("grp", "row")),
        P(),
        P("grp"),
        P(),
        P(),
    )
    return jax.shard_map(
        on_device,
        mesh=mesh,
        in_specs=placed,
        out_specs=P(("grp", "row"), None, None),
        check_vma=False,
    )
```

```python
import functools
import math

import jax
import jax.numpy as jnp
from jax import lax
from jax.experimental import pallas as pl
from jax.experimental.pallas import tpu as pltpu
from jax.sharding import PartitionSpec as P

CAP = 2
LANES = 128
CODE_ROWS = 8
VMEM = pltpu.MemorySpace.VMEM
SMEM = pltpu.MemorySpace.SMEM


def dot(a, b):
    return jnp.dot(a, b, preferred_element_type=jnp.float32)


def dot_nt(a, b):
    return lax.dot_general(a, b, (((1,), (1,)), ((), ())), preferred_element_type=jnp.float32)


def standardize(x):
    centred = x - jnp.mean(x, axis=-1, keepdims=True)
    variance = jnp.mean(centred * centred, axis=-1, keepdims=True)
    return centred * lax.rsqrt(variance + 1e-05)


def pack_kernel(n_devices, rows, x_ref, second_ref, tiles_ref, owner_ref, column_ref, send_ref, normed_ref, wide):
    depth, lines, _ = x_ref.shape
    slots, width = tiles_ref.shape
    tile_rows = width // LANES
    n_chan = second_ref.shape[0]
    right_rows = n_chan * depth // LANES
    x = x_ref[...].astype(jnp.float32)
    for t in range(lines):
        normed = standardize(x[:, t, :]).astype(jnp.bfloat16)
        normed_ref[pl.ds(t * depth, depth), :] = normed
        right = dot_nt(second_ref[...], normed)
        groups = n_chan // right_rows
        packed = jnp.concatenate(
            [right[b * right_rows : (b + 1) * right_rows] for b in range(groups)], axis=1
        )
        for d in range(n_devices):
            wide[pl.ds(d * rows + t * right_rows, right_rows), :] = packed
    owner = owner_ref[...]
    here = lax.broadcasted_iota(jnp.int32, (slots, slots), 0)
    there = lax.broadcasted_iota(jnp.int32, (slots, slots), 1)
    across = jnp.broadcast_to(owner, (slots, slots))
    down = jnp.sum(jnp.where(here == there, across, 0), axis=1, keepdims=True)
    rank = jnp.sum(jnp.where((down == across) & (here < there), 1, 0), axis=0, keepdims=True)
    target = rank * n_devices + owner
    place = lax.broadcasted_iota(jnp.int32, (CAP * n_devices, slots), 0) == target
    base = lines * right_rows
    code = jnp.where(place, (column_ref[...] + 1).astype(jnp.float32), 0.0)
    code = jnp.sum(code, axis=1, keepdims=True)
    code = jnp.broadcast_to(code, (CAP * n_devices, LANES))
    place = place.astype(jnp.bfloat16)
    for q in range(tile_rows):
        placed = dot(place, tiles_ref[:, q * LANES : (q + 1) * LANES])
        for c in range(CAP):
            wide[pl.ds(base + c * tile_rows + q, n_devices, stride=rows), :] = placed[
                c * n_devices : (c + 1) * n_devices
            ]
    base = base + CAP * tile_rows
    for c in range(CODE_ROWS):
        piece = min(c, CAP - 1)
        wide[pl.ds(base + c, n_devices, stride=rows), :] = code[piece * n_devices : (piece + 1) * n_devices]
    send_ref[...] = wide[...].astype(jnp.bfloat16)


def left_kernel(
    n_tiles, tc, normed_ref, first_ref, tensor_ref, lengths_ref, device_ref, folded_ref, same_ref
):
    n_chan = first_ref.shape[0]
    pair_chan = tensor_ref.shape[2]
    lines = folded_ref.shape[1] // pair_chan
    depth = normed_ref.shape[0] // lines
    left = dot_nt(normed_ref[...], first_ref[...]).astype(jnp.bfloat16)
    right_rows = n_chan * depth // LANES
    groups = n_chan // right_rows
    for d in range(n_chan):
        part = (dot(left, tensor_ref[d]) / depth).astype(jnp.bfloat16)
        at = (d % right_rows) * LANES + (d // right_rows) * depth
        for t in range(lines):
            folded_ref[pl.ds(at, depth), t * pair_chan : (t + 1) * pair_chan] = part[
                t * depth : (t + 1) * depth
            ]
    height, _ = same_ref.shape
    tile_rows = height // n_tiles
    per_row = tile_rows // lines
    packed = tc // per_row
    row = lax.broadcasted_iota(jnp.int32, same_ref.shape, 0)
    lane = lax.broadcasted_iota(jnp.int32, same_ref.shape, 1)
    column = (row // tile_rows) * tc + (row % per_row) * packed + lane // (LANES // packed)
    line = device_ref[0] * lines + (row % tile_rows) // per_row
    end = jnp.int32(0)
    column_chain = jnp.zeros_like(column)
    line_chain = jnp.zeros_like(line)
    for c in range(lengths_ref.shape[0]):
        end = end + lengths_ref[c]
        column_chain = column_chain + (column >= end).astype(jnp.int32)
        line_chain = line_chain + (line >= end).astype(jnp.int32)
    same_ref[...] = (column_chain == line_chain).astype(jnp.float32)


def pair_kernel(
    n_devices,
    rows,
    tc,
    got_ref,
    folded_ref,
    same_ref,
    offset_ref,
    structural_ref,
    sigmoid_ref,
    content_ref,
    out_ref,
    right_wide,
    sums,
    pair,
):
    n_temp, pair_chan = structural_ref.shape
    lines = folded_ref.shape[1] // pair_chan
    depth_chan = folded_ref.shape[0]
    right_rows = depth_chan // LANES
    n_tokens = n_devices * lines
    height = same_ref.shape[0]
    n_tiles = n_tokens // tc
    tile_rows = height // n_tiles
    base = lines * right_rows
    code_base = base + CAP * tile_rows

    sums[...] = jnp.zeros_like(sums)

    def add_source(d, carry):
        start = pl.multiple_of(d * rows, 8)
        right_wide[pl.ds(pl.multiple_of(d * base, 8), base), :] = got_ref[pl.ds(start, base), :].astype(
            jnp.float32
        )
        codes = got_ref[pl.ds(start + code_base, CODE_ROWS), :].astype(jnp.float32)
        counts = list(carry)
        for c in range(CAP):
            tile = got_ref[pl.ds(start + base + c * tile_rows, tile_rows), :].astype(jnp.float32)
            code = codes[c : c + 1, :]
            for k in range(n_tiles):
                hit = code == k + 1.0
                counts[k] = counts[k] + jnp.where(hit, 1.0, 0.0)
                at = pl.ds(k * tile_rows, tile_rows)
                sums[at, :] = sums[at, :] + jnp.where(hit, tile, 0.0)
        return tuple(counts)

    counts = tuple(jnp.zeros((1, LANES), jnp.float32) for _ in range(n_tiles))
    counts = lax.fori_loop(0, n_devices, add_source, counts, unroll=n_devices <= 16)
    for k in range(n_tiles):
        at = pl.ds(k * tile_rows, tile_rows)
        mean = sums[at, :] / jnp.maximum(counts[k], 1.0)
        template = (mean * same_ref[at, :]).astype(jnp.bfloat16)
        for h in range(LANES // n_temp):
            part = dot(template[:, h * n_temp : (h + 1) * n_temp], structural_ref[...])
            per_row = tile_rows // lines
            for t in range(lines):
                pair[pl.ds(t * n_tokens + k * tc + h, per_row, stride=LANES // n_temp), :] = part[
                    t * per_row : (t + 1) * per_row
                ]
    outer = None
    for g in range(right_rows):
        lhs = right_wide[pl.ds(g, n_tokens, stride=right_rows), :].astype(jnp.bfloat16)
        term = dot(lhs, folded_ref[pl.ds(g * LANES, LANES), :])
        outer = term if outer is None else outer + term
    for t in range(lines):
        at = pl.ds(t * n_tokens, n_tokens)
        total = pair[at, :] + (outer[:, t * pair_chan : (t + 1) * pair_chan] + offset_ref[...])
        pair_normed = standardize(total).astype(jnp.bfloat16)
        gate = jax.nn.sigmoid(dot(pair_normed, sigmoid_ref[...]))
        linear = dot(pair_normed, content_ref[...])
        out_ref[at, :] = (gate * linear).astype(out_ref.dtype)


def grant(*arrays):
    return pltpu.CompilerParams(
        vmem_limit_bytes=sum(2 * math.prod(shape) * jnp.dtype(kind).itemsize for shape, kind in arrays) + (1 << 20)
    )


def on_device(
    aligned_sequences,
    first_factor_matrix,
    second_factor_matrix,
    tensor_matrix,
    tensor_offset,
    structural_duplex_patches,
    patch_source_index,
    patch_target_index,
    structural_matrix,
    polymer_residue_lengths,
    sigmoid_matrix,
    content_matrix,
):
    n_devices = lax.axis_size("row")
    device_id = lax.axis_index("row")
    depth, lines, n_feat = aligned_sequences.shape
    slots, width = structural_duplex_patches.shape
    n_chan = first_factor_matrix.shape[1]
    n_temp, pair_chan = structural_matrix.shape
    tc = width // (lines * n_temp)
    n_tokens = lines * n_devices
    n_tiles = n_tokens // tc
    tile_rows = width // LANES
    right_rows = n_chan * depth // LANES
    rows = lines * right_rows + CAP * tile_rows + CODE_ROWS
    vmem = pl.BlockSpec(memory_space=VMEM)
    smem = pl.BlockSpec(memory_space=SMEM)

    send, normed = pl.pallas_call(
        functools.partial(pack_kernel, n_devices, rows),
        out_shape=(
            jax.ShapeDtypeStruct((n_devices * rows, LANES), jnp.bfloat16),
            jax.ShapeDtypeStruct((lines * depth, n_feat), jnp.bfloat16),
        ),
        in_specs=[vmem] * 5,
        out_specs=(vmem, vmem),
        scratch_shapes=[pltpu.VMEM((n_devices * rows, LANES), jnp.float32)],
    )(
        aligned_sequences,
        second_factor_matrix.T,
        structural_duplex_patches,
        patch_source_index.reshape(1, slots),
        patch_target_index.reshape(1, slots),
    )
    got = lax.all_to_all(
        send.reshape(n_devices, rows, LANES), "row", split_axis=0, concat_axis=0, tiled=True
    ).reshape(n_devices * rows, LANES)
    folded, same = pl.pallas_call(
        functools.partial(left_kernel, n_tiles, tc),
        out_shape=(
            jax.ShapeDtypeStruct((n_chan * depth, lines * pair_chan), jnp.bfloat16),
            jax.ShapeDtypeStruct((n_tiles * tile_rows, LANES), jnp.float32),
        ),
        in_specs=[vmem] * 3 + [smem] * 2,
        out_specs=(vmem, vmem),
        compiler_params=grant(
            ((n_chan * n_chan, pair_chan), jnp.bfloat16),
            ((n_chan * depth, lines * pair_chan), jnp.bfloat16),
            ((n_tiles * tile_rows, LANES), jnp.float32),
        ),
    )(
        normed,
        first_factor_matrix.T,
        tensor_matrix.reshape(n_chan, n_chan, pair_chan).transpose(1, 0, 2),
        polymer_residue_lengths,
        device_id.reshape(1),
    )
    out = pl.pallas_call(
        functools.partial(pair_kernel, n_devices, rows, tc),
        out_shape=jax.ShapeDtypeStruct((lines * n_tokens, pair_chan), jnp.bfloat16),
        in_specs=[vmem] * 7,
        out_specs=vmem,
        scratch_shapes=[
            pltpu.VMEM((n_devices * lines * right_rows, LANES), jnp.float32),
            pltpu.VMEM((n_tiles * tile_rows, LANES), jnp.float32),
            pltpu.VMEM((lines * n_tokens, pair_chan), jnp.float32),
        ],
        compiler_params=grant(
            ((n_devices * rows, LANES), jnp.bfloat16),
            ((n_chan * depth, lines * pair_chan), jnp.bfloat16),
            ((n_devices * lines * right_rows, LANES), jnp.float32),
            ((2 * n_tiles * tile_rows, LANES), jnp.float32),
            ((2 * lines * n_tokens, pair_chan), jnp.float32),
        ),
    )(
        got,
        folded,
        same,
        tensor_offset.astype(jnp.float32).reshape(1, pair_chan),
        structural_matrix,
        sigmoid_matrix,
        content_matrix,
    )
    return out.reshape(lines, n_tokens, pair_chan)


def solution(mesh):
    placed = (
        P(None, ("grp", "row"), None),
        P(),
        P(),
        P(),
        P(),
        P(("grp", "row"), None),
        P(("grp", "row"), None),
        P(("grp", "row")),
        P(),
        P("grp"),
        P(),
        P(),
    )
    return jax.shard_map(
        on_device,
        mesh=mesh,
        in_specs=placed,
        out_specs=P(("grp", "row"), None, None),
        check_vma=False,
    )
```

```python
import functools
import math

import jax
import jax.numpy as jnp
from jax import lax
from jax.experimental import pallas as pl
from jax.experimental.pallas import tpu as pltpu
from jax.sharding import PartitionSpec as P

CAP = 2
LANES = 128
VMEM = pltpu.MemorySpace.VMEM
SMEM = pltpu.MemorySpace.SMEM


def dot(a, b):
    return jnp.dot(a, b, preferred_element_type=jnp.float32)


def dot_nt(a, b):
    return lax.dot_general(a, b, (((1,), (1,)), ((), ())), preferred_element_type=jnp.float32)


def standardize(x):
    centred = x - jnp.mean(x, axis=-1, keepdims=True)
    variance = jnp.mean(centred * centred, axis=-1, keepdims=True)
    return centred * lax.rsqrt(variance + 1e-05)


def pack_kernel(
    n_devices,
    rows,
    x_hbm,
    second_hbm,
    tiles_hbm,
    owner_hbm,
    column_hbm,
    send_ref,
    normed_ref,
    x_ref,
    second_ref,
    tiles_ref,
    owner_ref,
    column_ref,
    wide,
    arrived,
):
    loads = [
        pltpu.make_async_copy(source, target, arrived.at[n])
        for n, (source, target) in enumerate(
            (
                (owner_hbm, owner_ref),
                (column_hbm, column_ref),
                (x_hbm, x_ref),
                (second_hbm, second_ref),
                (tiles_hbm, tiles_ref),
            )
        )
    ]
    for load in loads:
        load.start()
    depth, lines, _ = x_ref.shape
    slots, width = tiles_ref.shape
    tile_rows = width // LANES
    n_chan = second_ref.shape[0]
    right_rows = n_chan * depth // LANES
    base = lines * right_rows
    here = lax.broadcasted_iota(jnp.int32, (slots, slots), 0)
    there = lax.broadcasted_iota(jnp.int32, (slots, slots), 1)
    for load in loads[:2]:
        load.wait()
    across = jnp.broadcast_to(owner_ref[...], (slots, slots))
    down = jnp.sum(jnp.where(here == there, across, 0), axis=1, keepdims=True)
    rank = jnp.sum(jnp.where((down == across) & (here < there), 1, 0), axis=0, keepdims=True)
    target = rank * n_devices + owner_ref[...]
    place = lax.broadcasted_iota(jnp.int32, (CAP * n_devices, slots), 0) == target
    code = jnp.where(place, (column_ref[...] + 1).astype(jnp.float32), 0.0)
    code = jnp.broadcast_to(jnp.sum(code, axis=1, keepdims=True), (CAP * n_devices, LANES))
    for c in range(CAP):
        wide[pl.ds(base + CAP * tile_rows + c, n_devices, stride=rows), :] = code[
            c * n_devices : (c + 1) * n_devices
        ]
    for load in loads[2:]:
        load.wait()
    x = x_ref[...].astype(jnp.float32)
    for t in range(lines):
        normed = standardize(x[:, t, :]).astype(jnp.bfloat16)
        normed_ref[pl.ds(t * depth, depth), :] = normed
        right = dot_nt(second_ref[...], normed)
        groups = n_chan // right_rows
        packed = jnp.concatenate(
            [right[b * right_rows : (b + 1) * right_rows] for b in range(groups)], axis=1
        )
        for d in range(n_devices):
            wide[pl.ds(d * rows + t * right_rows, right_rows), :] = packed
    place = place.astype(jnp.bfloat16)
    for q in range(tile_rows):
        placed = dot(place, tiles_ref[:, q * LANES : (q + 1) * LANES])
        for c in range(CAP):
            wide[pl.ds(base + c * tile_rows + q, n_devices, stride=rows), :] = placed[
                c * n_devices : (c + 1) * n_devices
            ]
    send_ref[...] = wide[...].astype(jnp.bfloat16)


def left_kernel(
    n_tiles, tc, normed_ref, first_ref, tensor_ref, lengths_ref, device_ref, folded_ref, same_ref
):
    n_chan = first_ref.shape[0]
    pair_chan = tensor_ref.shape[2]
    lines = folded_ref.shape[1] // pair_chan
    depth = normed_ref.shape[0] // lines
    left = dot_nt(normed_ref[...], first_ref[...]).astype(jnp.bfloat16)
    right_rows = n_chan * depth // LANES
    groups = n_chan // right_rows
    for d in range(n_chan):
        part = (dot(left, tensor_ref[d]) / depth).astype(jnp.bfloat16)
        at = (d % right_rows) * LANES + (d // right_rows) * depth
        for t in range(lines):
            folded_ref[pl.ds(at, depth), t * pair_chan : (t + 1) * pair_chan] = part[
                t * depth : (t + 1) * depth
            ]
    height, _ = same_ref.shape
    tile_rows = height // n_tiles
    per_row = tile_rows // lines
    packed = tc // per_row
    row = lax.broadcasted_iota(jnp.int32, same_ref.shape, 0)
    lane = lax.broadcasted_iota(jnp.int32, same_ref.shape, 1)
    column = (row // tile_rows) * tc + (row % per_row) * packed + lane // (LANES // packed)
    line = device_ref[0] * lines + (row % tile_rows) // per_row
    end = jnp.int32(0)
    column_chain = jnp.zeros_like(column)
    line_chain = jnp.zeros_like(line)
    for c in range(lengths_ref.shape[0]):
        end = end + lengths_ref[c]
        column_chain = column_chain + (column >= end).astype(jnp.int32)
        line_chain = line_chain + (line >= end).astype(jnp.int32)
    same_ref[...] = (column_chain == line_chain).astype(jnp.float32)


def pair_kernel(
    n_devices,
    rows,
    tc,
    got_ref,
    folded_ref,
    same_ref,
    offset_ref,
    structural_ref,
    sigmoid_ref,
    content_ref,
    out_ref,
    wide,
    sums,
    pair,
    final,
):
    n_temp, pair_chan = structural_ref.shape
    lines = folded_ref.shape[1] // pair_chan
    right_rows = folded_ref.shape[0] // LANES
    n_tokens = n_devices * lines
    n_tiles = n_tokens // tc
    tile_rows = same_ref.shape[0] // n_tiles
    base = lines * right_rows
    wide[...] = got_ref[...].astype(jnp.float32)

    unrolled = n_devices <= 16
    if not unrolled:
        sums[...] = jnp.zeros_like(sums)

    def add_source(d, carry):
        start = d * rows
        counts, totals = carry
        for c in range(CAP):
            tile = wide[pl.ds(start + base + c * tile_rows, tile_rows), :]
            code = wide[pl.ds(start + base + CAP * tile_rows + c, 1), :]
            for k in range(n_tiles):
                hit = code == k + 1.0
                counts[k] = counts[k] + jnp.where(hit, 1.0, 0.0)
                term = jnp.where(hit, tile, 0.0)
                if unrolled:
                    totals[k] = term if totals[k] is None else totals[k] + term
                else:
                    at = pl.ds(k * tile_rows, tile_rows)
                    sums[at, :] = sums[at, :] + term
        return counts, totals

    counts = [jnp.zeros((1, LANES), jnp.float32) for _ in range(n_tiles)]
    totals = [None] * n_tiles
    if unrolled:
        for d in range(n_devices):
            counts, totals = add_source(d, (counts, totals))
    else:
        counts = lax.fori_loop(0, n_devices, lambda d, kept: add_source(d, (kept, totals))[0], counts)
        totals = [sums[pl.ds(k * tile_rows, tile_rows), :] for k in range(n_tiles)]
    outer = None
    for g in range(right_rows):
        lhs = jnp.concatenate(
            [wide[pl.ds(t * right_rows + g, n_devices, stride=rows), :] for t in range(lines)], axis=0
        ).astype(jnp.bfloat16)
        term = dot(lhs, folded_ref[pl.ds(g * LANES, LANES), :])
        outer = term if outer is None else outer + term
    packed = LANES // n_temp
    per_row = tile_rows // lines
    for k in range(n_tiles):
        at = pl.ds(k * tile_rows, tile_rows)
        mean = totals[k] / jnp.maximum(counts[k], 1.0)
        template = (mean * same_ref[at, :]).astype(jnp.bfloat16)
        for h in range(packed):
            part = dot(template[:, h * n_temp : (h + 1) * n_temp], structural_ref[...])
            for i in range(lines):
                if packed == lines:
                    where = pl.ds(i * n_tokens + h * n_devices + k * per_row, per_row)
                else:
                    first = k * tc + h
                    where = pl.ds(
                        i * n_tokens + (first % lines) * n_devices + first // lines,
                        per_row,
                        stride=packed // lines,
                    )
                pair[where, :] = part[i * per_row : (i + 1) * per_row]
    for i in range(lines):
        at = pl.ds(i * n_tokens, n_tokens)
        total = pair[at, :] + (outer[:, i * pair_chan : (i + 1) * pair_chan] + offset_ref[...])
        pair_normed = standardize(total).astype(jnp.bfloat16)
        gate = jax.nn.sigmoid(dot(pair_normed, sigmoid_ref[...]))
        linear = dot(pair_normed, content_ref[...])
        result = gate * linear
        for t in range(lines):
            final[pl.ds(i * n_tokens + t, n_devices, stride=lines), :] = result[
                t * n_devices : (t + 1) * n_devices
            ]
    out_ref[...] = final[...].astype(out_ref.dtype)


def grant(*arrays):
    return pltpu.CompilerParams(
        vmem_limit_bytes=sum(2 * math.prod(shape) * jnp.dtype(kind).itemsize for shape, kind in arrays) + (1 << 20)
    )


def on_device(
    aligned_sequences,
    first_factor_matrix,
    second_factor_matrix,
    tensor_matrix,
    tensor_offset,
    structural_duplex_patches,
    patch_source_index,
    patch_target_index,
    structural_matrix,
    polymer_residue_lengths,
    sigmoid_matrix,
    content_matrix,
):
    n_devices = lax.axis_size("row")
    device_id = lax.axis_index("row")
    depth, lines, n_feat = aligned_sequences.shape
    slots, width = structural_duplex_patches.shape
    n_chan = first_factor_matrix.shape[1]
    n_temp, pair_chan = structural_matrix.shape
    tc = width // (lines * n_temp)
    n_tokens = lines * n_devices
    n_tiles = n_tokens // tc
    tile_rows = width // LANES
    right_rows = n_chan * depth // LANES
    rows = lines * right_rows + CAP * tile_rows + CAP
    vmem = pl.BlockSpec(memory_space=VMEM)
    smem = pl.BlockSpec(memory_space=SMEM)
    hbm = pl.BlockSpec(memory_space=pltpu.MemorySpace.HBM)

    send, normed = pl.pallas_call(
        functools.partial(pack_kernel, n_devices, rows),
        out_shape=(
            jax.ShapeDtypeStruct((n_devices * rows, LANES), jnp.bfloat16),
            jax.ShapeDtypeStruct((lines * depth, n_feat), jnp.bfloat16),
        ),
        in_specs=[hbm] * 5,
        out_specs=(vmem, vmem),
        scratch_shapes=[
            pltpu.VMEM(aligned_sequences.shape, jnp.bfloat16),
            pltpu.VMEM((n_chan, n_feat), jnp.bfloat16),
            pltpu.VMEM((slots, width), jnp.bfloat16),
            pltpu.VMEM((1, slots), jnp.int32),
            pltpu.VMEM((1, slots), jnp.int32),
            pltpu.VMEM((n_devices * rows, LANES), jnp.float32),
            pltpu.SemaphoreType.DMA((5,)),
        ],
    )(
        aligned_sequences,
        second_factor_matrix.T,
        structural_duplex_patches,
        patch_source_index.reshape(1, slots),
        patch_target_index.reshape(1, slots),
    )
    got = lax.all_to_all(
        send.reshape(n_devices, rows // 2, 2, LANES), "row", split_axis=0, concat_axis=0, tiled=True
    ).reshape(n_devices * rows, LANES)
    folded, same = pl.pallas_call(
        functools.partial(left_kernel, n_tiles, tc),
        out_shape=(
            jax.ShapeDtypeStruct((n_chan * depth, lines * pair_chan), jnp.bfloat16),
            jax.ShapeDtypeStruct((n_tiles * tile_rows, LANES), jnp.float32),
        ),
        in_specs=[vmem] * 3 + [smem] * 2,
        out_specs=(vmem, vmem),
        compiler_params=grant(
            ((n_chan * n_chan, pair_chan), jnp.bfloat16),
            ((n_chan * depth, lines * pair_chan), jnp.bfloat16),
            ((n_tiles * tile_rows, LANES), jnp.float32),
        ),
    )(
        normed,
        first_factor_matrix.T,
        tensor_matrix.reshape(n_chan, n_chan, pair_chan).transpose(1, 0, 2),
        polymer_residue_lengths,
        device_id.reshape(1),
    )
    out = pl.pallas_call(
        functools.partial(pair_kernel, n_devices, rows, tc),
        out_shape=jax.ShapeDtypeStruct((lines * n_tokens, pair_chan), jnp.bfloat16),
        in_specs=[vmem] * 7,
        out_specs=vmem,
        scratch_shapes=[
            pltpu.VMEM((n_devices * rows, LANES), jnp.float32),
            pltpu.VMEM((n_tiles * tile_rows, LANES), jnp.float32),
            pltpu.VMEM((lines * n_tokens, pair_chan), jnp.float32),
            pltpu.VMEM((lines * n_tokens, pair_chan), jnp.float32),
        ],
        compiler_params=grant(
            ((n_devices * rows, LANES), jnp.bfloat16),
            ((n_chan * depth, lines * pair_chan), jnp.bfloat16),
            ((n_devices * rows, LANES), jnp.float32),
            ((2 * n_tiles * tile_rows, LANES), jnp.float32),
            ((3 * lines * n_tokens, pair_chan), jnp.float32),
        ),
    )(
        got,
        folded,
        same,
        tensor_offset.astype(jnp.float32).reshape(1, pair_chan),
        structural_matrix,
        sigmoid_matrix,
        content_matrix,
    )
    return out.reshape(lines, n_tokens, pair_chan)


def solution(mesh):
    placed = (
        P(None, ("grp", "row"), None),
        P(),
        P(),
        P(),
        P(),
        P(("grp", "row"), None),
        P(("grp", "row"), None),
        P(("grp", "row")),
        P(),
        P("grp"),
        P(),
        P(),
    )
    return jax.shard_map(
        on_device,
        mesh=mesh,
        in_specs=placed,
        out_specs=P(("grp", "row"), None, None),
        check_vma=False,
    )
```

```python
import functools
import math

import jax
import jax.numpy as jnp
from jax import lax
from jax.experimental import pallas as pl
from jax.experimental.pallas import tpu as pltpu
from jax.sharding import PartitionSpec as P

CAP = 2
LANES = 128
ORDERS = {16: (8, 3, 5, 2, 15, 7, 12, 4, 14, 13, 10, 1, 6, 11, 0, 9)}
VMEM = pltpu.MemorySpace.VMEM
SMEM = pltpu.MemorySpace.SMEM


def dot(a, b):
    return jnp.dot(a, b, preferred_element_type=jnp.float32)


def dot_nt(a, b):
    return lax.dot_general(a, b, (((1,), (1,)), ((), ())), preferred_element_type=jnp.float32)


def exchange_order(n_devices):
    return ORDERS.get(n_devices, tuple(range(n_devices)))


def store_rows(ref, places, value):
    step = places[1] - places[0]
    if step > 0 and all(b - a == step for a, b in zip(places, places[1:])):
        ref[pl.ds(places[0], len(places), stride=step), :] = value
    else:
        for n, place in enumerate(places):
            ref[pl.ds(place, 1), :] = value[n : n + 1]


def standardize(x):
    centred = x - jnp.mean(x, axis=-1, keepdims=True)
    variance = jnp.mean(centred * centred, axis=-1, keepdims=True)
    return centred * lax.rsqrt(variance + 1e-05)


def pack_kernel(
    n_devices,
    rows,
    x_hbm,
    second_hbm,
    tiles_hbm,
    owner_hbm,
    column_hbm,
    send_ref,
    normed_ref,
    x_ref,
    second_ref,
    tiles_ref,
    owner_ref,
    column_ref,
    wide,
    arrived,
):
    loads = [
        pltpu.make_async_copy(source, target, arrived.at[n])
        for n, (source, target) in enumerate(
            (
                (owner_hbm, owner_ref),
                (column_hbm, column_ref),
                (x_hbm, x_ref),
                (second_hbm, second_ref),
                (tiles_hbm, tiles_ref),
            )
        )
    ]
    for load in loads:
        load.start()
    depth, lines, _ = x_ref.shape
    slots, width = tiles_ref.shape
    tile_rows = width // LANES
    n_chan = second_ref.shape[0]
    right_rows = n_chan * depth // LANES
    base = lines * right_rows
    here = lax.broadcasted_iota(jnp.int32, (slots, slots), 0)
    there = lax.broadcasted_iota(jnp.int32, (slots, slots), 1)
    order = exchange_order(n_devices)
    slot = lax.broadcasted_iota(jnp.int32, (CAP * n_devices, slots), 0)
    if order != tuple(range(n_devices)):
        position = slot % n_devices
        device = jnp.zeros_like(slot)
        for p, d in enumerate(order):
            device = jnp.where(position == p, d, device)
        slot = slot - position + device
    for load in loads[:2]:
        load.wait()
    across = jnp.broadcast_to(owner_ref[...], (slots, slots))
    down = jnp.sum(jnp.where(here == there, across, 0), axis=1, keepdims=True)
    rank = jnp.sum(jnp.where((down == across) & (here < there), 1, 0), axis=0, keepdims=True)
    target = rank * n_devices + owner_ref[...]
    place = slot == target
    code = jnp.where(place, (column_ref[...] + 1).astype(jnp.float32), 0.0)
    code = jnp.broadcast_to(jnp.sum(code, axis=1, keepdims=True), (CAP * n_devices, LANES))
    for c in range(CAP):
        wide[pl.ds(base + CAP * tile_rows + c, n_devices, stride=rows), :] = code[
            c * n_devices : (c + 1) * n_devices
        ]
    for load in loads[2:]:
        load.wait()
    x = x_ref[...].astype(jnp.float32)
    for t in range(lines):
        normed = standardize(x[:, t, :]).astype(jnp.bfloat16)
        normed_ref[pl.ds(t * depth, depth), :] = normed
        right = dot_nt(second_ref[...], normed)
        groups = n_chan // right_rows
        packed = jnp.concatenate(
            [right[b * right_rows : (b + 1) * right_rows] for b in range(groups)], axis=1
        )
        for d in range(n_devices):
            wide[pl.ds(d * rows + t * right_rows, right_rows), :] = packed
    place = place.astype(jnp.bfloat16)
    for q in range(tile_rows):
        placed = dot(place, tiles_ref[:, q * LANES : (q + 1) * LANES])
        for c in range(CAP):
            wide[pl.ds(base + c * tile_rows + q, n_devices, stride=rows), :] = placed[
                c * n_devices : (c + 1) * n_devices
            ]
    send_ref[...] = wide[...].astype(jnp.bfloat16)


def left_kernel(
    n_tiles, tc, normed_ref, first_ref, tensor_ref, lengths_ref, device_ref, folded_ref, same_ref
):
    n_chan = first_ref.shape[0]
    pair_chan = tensor_ref.shape[2]
    lines = folded_ref.shape[1] // pair_chan
    depth = normed_ref.shape[0] // lines
    left = dot_nt(normed_ref[...], first_ref[...]).astype(jnp.bfloat16)
    right_rows = n_chan * depth // LANES
    groups = n_chan // right_rows
    for d in range(n_chan):
        part = (dot(left, tensor_ref[d]) / depth).astype(jnp.bfloat16)
        at = (d % right_rows) * LANES + (d // right_rows) * depth
        for t in range(lines):
            folded_ref[pl.ds(at, depth), t * pair_chan : (t + 1) * pair_chan] = part[
                t * depth : (t + 1) * depth
            ]
    height, _ = same_ref.shape
    tile_rows = height // n_tiles
    per_row = tile_rows // lines
    packed = tc // per_row
    row = lax.broadcasted_iota(jnp.int32, same_ref.shape, 0)
    lane = lax.broadcasted_iota(jnp.int32, same_ref.shape, 1)
    column = (row // tile_rows) * tc + (row % per_row) * packed + lane // (LANES // packed)
    line = device_ref[0] * lines + (row % tile_rows) // per_row
    end = jnp.int32(0)
    column_chain = jnp.zeros_like(column)
    line_chain = jnp.zeros_like(line)
    for c in range(lengths_ref.shape[0]):
        end = end + lengths_ref[c]
        column_chain = column_chain + (column >= end).astype(jnp.int32)
        line_chain = line_chain + (line >= end).astype(jnp.int32)
    same_ref[...] = (column_chain == line_chain).astype(jnp.float32)


def pair_kernel(
    n_devices,
    rows,
    tc,
    got_ref,
    folded_ref,
    same_ref,
    offset_ref,
    structural_ref,
    sigmoid_ref,
    content_ref,
    out_ref,
    wide,
    sums,
    pair,
    opm,
):
    n_temp, pair_chan = structural_ref.shape
    lines = folded_ref.shape[1] // pair_chan
    right_rows = folded_ref.shape[0] // LANES
    n_tokens = n_devices * lines
    n_tiles = n_tokens // tc
    tile_rows = same_ref.shape[0] // n_tiles
    base = lines * right_rows
    wide[...] = got_ref[...].astype(jnp.float32)

    unrolled = n_devices <= 16
    if not unrolled:
        sums[...] = jnp.zeros_like(sums)

    def add_source(d, carry):
        start = d * rows
        counts, totals = carry
        for c in range(CAP):
            tile = wide[pl.ds(start + base + c * tile_rows, tile_rows), :]
            code = wide[pl.ds(start + base + CAP * tile_rows + c, 1), :]
            for k in range(n_tiles):
                hit = code == k + 1.0
                counts[k] = counts[k] + jnp.where(hit, 1.0, 0.0)
                term = jnp.where(hit, tile, 0.0)
                if unrolled:
                    totals[k] = term if totals[k] is None else totals[k] + term
                else:
                    at = pl.ds(k * tile_rows, tile_rows)
                    sums[at, :] = sums[at, :] + term
        return counts, totals

    counts = [jnp.zeros((1, LANES), jnp.float32) for _ in range(n_tiles)]
    totals = [None] * n_tiles
    if unrolled:
        for d in range(n_devices):
            counts, totals = add_source(d, (counts, totals))
    else:
        counts = lax.fori_loop(0, n_devices, lambda d, kept: add_source(d, (kept, totals))[0], counts)
        totals = [sums[pl.ds(k * tile_rows, tile_rows), :] for k in range(n_tiles)]
    outer = None
    for g in range(right_rows):
        lhs = jnp.concatenate(
            [wide[pl.ds(t * right_rows + g, n_devices, stride=rows), :] for t in range(lines)], axis=0
        ).astype(jnp.bfloat16)
        term = dot(lhs, folded_ref[pl.ds(g * LANES, LANES), :])
        outer = term if outer is None else outer + term
    order = exchange_order(n_devices)
    for i in range(lines):
        for t in range(lines):
            store_rows(
                opm,
                [i * n_tokens + d * lines + t for d in order],
                outer[t * n_devices : (t + 1) * n_devices, i * pair_chan : (i + 1) * pair_chan],
            )
    packed = LANES // n_temp
    per_row = tile_rows // lines
    for k in range(n_tiles):
        at = pl.ds(k * tile_rows, tile_rows)
        mean = totals[k] / jnp.maximum(counts[k], 1.0)
        template = (mean * same_ref[at, :]).astype(jnp.bfloat16)
        for h in range(packed):
            part = dot(template[:, h * n_temp : (h + 1) * n_temp], structural_ref[...])
            for i in range(lines):
                first = i * n_tokens + k * tc + h
                pair[pl.ds(first, per_row, stride=packed), :] = part[i * per_row : (i + 1) * per_row]
    for i in range(lines):
        at = pl.ds(i * n_tokens, n_tokens)
        total = pair[at, :] + (opm[at, :] + offset_ref[...])
        pair_normed = standardize(total).astype(jnp.bfloat16)
        gate = jax.nn.sigmoid(dot(pair_normed, sigmoid_ref[...]))
        linear = dot(pair_normed, content_ref[...])
        out_ref[at, :] = (gate * linear).astype(out_ref.dtype)


def grant(*arrays):
    return pltpu.CompilerParams(
        vmem_limit_bytes=sum(2 * math.prod(shape) * jnp.dtype(kind).itemsize for shape, kind in arrays) + (1 << 20)
    )


def on_device(
    aligned_sequences,
    first_factor_matrix,
    second_factor_matrix,
    tensor_matrix,
    tensor_offset,
    structural_duplex_patches,
    patch_source_index,
    patch_target_index,
    structural_matrix,
    polymer_residue_lengths,
    sigmoid_matrix,
    content_matrix,
):
    n_devices = lax.axis_size("row")
    device_id = lax.axis_index("row")
    depth, lines, n_feat = aligned_sequences.shape
    slots, width = structural_duplex_patches.shape
    n_chan = first_factor_matrix.shape[1]
    n_temp, pair_chan = structural_matrix.shape
    tc = width // (lines * n_temp)
    n_tokens = lines * n_devices
    n_tiles = n_tokens // tc
    tile_rows = width // LANES
    right_rows = n_chan * depth // LANES
    rows = lines * right_rows + CAP * tile_rows + CAP
    vmem = pl.BlockSpec(memory_space=VMEM)
    smem = pl.BlockSpec(memory_space=SMEM)
    hbm = pl.BlockSpec(memory_space=pltpu.MemorySpace.HBM)

    send, normed = pl.pallas_call(
        functools.partial(pack_kernel, n_devices, rows),
        out_shape=(
            jax.ShapeDtypeStruct((n_devices * rows, LANES), jnp.bfloat16),
            jax.ShapeDtypeStruct((lines * depth, n_feat), jnp.bfloat16),
        ),
        in_specs=[hbm] * 5,
        out_specs=(vmem, vmem),
        scratch_shapes=[
            pltpu.VMEM(aligned_sequences.shape, jnp.bfloat16),
            pltpu.VMEM((n_chan, n_feat), jnp.bfloat16),
            pltpu.VMEM((slots, width), jnp.bfloat16),
            pltpu.VMEM((1, slots), jnp.int32),
            pltpu.VMEM((1, slots), jnp.int32),
            pltpu.VMEM((n_devices * rows, LANES), jnp.float32),
            pltpu.SemaphoreType.DMA((5,)),
        ],
    )(
        aligned_sequences,
        second_factor_matrix.T,
        structural_duplex_patches,
        patch_source_index.reshape(1, slots),
        patch_target_index.reshape(1, slots),
    )
    got = lax.all_to_all(
        send.reshape(n_devices, rows // 2, 2, LANES),
        "row",
        split_axis=0, concat_axis=0, tiled=True,
        axis_index_groups=[exchange_order(n_devices)],
    ).reshape(n_devices * rows, LANES)
    folded, same = pl.pallas_call(
        functools.partial(left_kernel, n_tiles, tc),
        out_shape=(
            jax.ShapeDtypeStruct((n_chan * depth, lines * pair_chan), jnp.bfloat16),
            jax.ShapeDtypeStruct((n_tiles * tile_rows, LANES), jnp.float32),
        ),
        in_specs=[vmem] * 3 + [smem] * 2,
        out_specs=(vmem, vmem),
        compiler_params=grant(
            ((n_chan * n_chan, pair_chan), jnp.bfloat16),
            ((n_chan * depth, lines * pair_chan), jnp.bfloat16),
            ((n_tiles * tile_rows, LANES), jnp.float32),
        ),
    )(
        normed,
        first_factor_matrix.T,
        tensor_matrix.reshape(n_chan, n_chan, pair_chan).transpose(1, 0, 2),
        polymer_residue_lengths,
        device_id.reshape(1),
    )
    out = pl.pallas_call(
        functools.partial(pair_kernel, n_devices, rows, tc),
        out_shape=jax.ShapeDtypeStruct((lines * n_tokens, pair_chan), jnp.bfloat16),
        in_specs=[vmem] * 7,
        out_specs=vmem,
        scratch_shapes=[
            pltpu.VMEM((n_devices * rows, LANES), jnp.float32),
            pltpu.VMEM((n_tiles * tile_rows, LANES), jnp.float32),
            pltpu.VMEM((lines * n_tokens, pair_chan), jnp.float32),
            pltpu.VMEM((lines * n_tokens, pair_chan), jnp.float32),
        ],
        compiler_params=grant(
            ((n_devices * rows, LANES), jnp.bfloat16),
            ((n_chan * depth, lines * pair_chan), jnp.bfloat16),
            ((n_devices * rows, LANES), jnp.float32),
            ((2 * n_tiles * tile_rows, LANES), jnp.float32),
            ((3 * lines * n_tokens, pair_chan), jnp.float32),
        ),
    )(
        got,
        folded,
        same,
        tensor_offset.astype(jnp.float32).reshape(1, pair_chan),
        structural_matrix,
        sigmoid_matrix,
        content_matrix,
    )
    return out.reshape(lines, n_tokens, pair_chan)


def solution(mesh):
    placed = (
        P(None, ("grp", "row"), None),
        P(),
        P(),
        P(),
        P(),
        P(("grp", "row"), None),
        P(("grp", "row"), None),
        P(("grp", "row")),
        P(),
        P("grp"),
        P(),
        P(),
    )
    return jax.shard_map(
        on_device,
        mesh=mesh,
        in_specs=placed,
        out_specs=P(("grp", "row"), None, None),
        check_vma=False,
    )
```

```python
import functools
import math

import jax
import jax.numpy as jnp
from jax import lax
from jax.experimental import pallas as pl
from jax.experimental.pallas import tpu as pltpu
from jax.sharding import PartitionSpec as P

CAP = 2
LANES = 128
ORDERS = {16: (8, 3, 5, 2, 15, 7, 12, 4, 14, 13, 10, 1, 6, 11, 0, 9)}
VMEM = pltpu.MemorySpace.VMEM
HBM = pltpu.MemorySpace.HBM


def dot(a, b):
    return jnp.dot(a, b, preferred_element_type=jnp.float32)


def dot_nt(a, b):
    return lax.dot_general(a, b, (((1,), (1,)), ((), ())), preferred_element_type=jnp.float32)


def exchange_order(n_devices):
    return ORDERS.get(n_devices, tuple(range(n_devices)))


def store_rows(ref, places, value):
    step = places[1] - places[0]
    if step > 0 and all(b - a == step for a, b in zip(places, places[1:])):
        ref[pl.ds(places[0], len(places), stride=step), :] = value
    else:
        for n, place in enumerate(places):
            ref[pl.ds(place, 1), :] = value[n : n + 1]


def standardize(x):
    centred = x - jnp.mean(x, axis=-1, keepdims=True)
    variance = jnp.mean(centred * centred, axis=-1, keepdims=True)
    return centred * lax.rsqrt(variance + 1e-05)


def pack_kernel(n_devices, rows, tc, n_loads, *refs):
    (
        x_hbm,
        second_hbm,
        tiles_hbm,
        owner_hbm,
        column_hbm,
        first_hbm,
        lengths_hbm,
        tensor_hbm,
        offset_hbm,
        structural_hbm,
        sigmoid_hbm,
        content_hbm,
        send_ref,
        left_ref,
        same_ref,
        tensor_ref,
        offset_ref,
        structural_ref,
        sigmoid_ref,
        content_ref,
        x_ref,
        second_ref,
        tiles_ref,
        owner_ref,
        column_ref,
        first_ref,
        lengths_ref,
        wide,
        arrived,
    ) = refs
    pairs = tensor_ref.shape[0]
    copies = [
        (owner_hbm, owner_ref),
        (column_hbm, column_ref),
        (x_hbm, x_ref),
        (second_hbm, second_ref),
        (tiles_hbm, tiles_ref),
        (lengths_hbm, lengths_ref),
        (first_hbm, first_ref),
        (offset_hbm, offset_ref),
        (structural_hbm, structural_ref),
        (sigmoid_hbm, sigmoid_ref),
        (content_hbm, content_ref),
    ] + [(tensor_hbm.at[:, p], tensor_ref.at[p]) for p in range(pairs)]
    loads = [pltpu.make_async_copy(source, target, arrived.at[n]) for n, (source, target) in enumerate(copies)]
    for load in loads:
        load.start()
    depth, lines, _ = x_ref.shape
    slots, width = tiles_ref.shape
    tile_rows = width // LANES
    n_chan = second_ref.shape[0]
    right_rows = n_chan * depth // LANES
    base = lines * right_rows
    here = lax.broadcasted_iota(jnp.int32, (slots, slots), 0)
    there = lax.broadcasted_iota(jnp.int32, (slots, slots), 1)
    order = exchange_order(n_devices)
    slot = lax.broadcasted_iota(jnp.int32, (CAP * n_devices, slots), 0)
    if order != tuple(range(n_devices)):
        position = slot % n_devices
        device = jnp.zeros_like(slot)
        for p, d in enumerate(order):
            device = jnp.where(position == p, d, device)
        slot = slot - position + device
    spread_row = lax.broadcasted_iota(jnp.int32, (4 * n_chan, n_chan), 0)
    spread_chan = lax.broadcasted_iota(jnp.int32, (4 * n_chan, n_chan), 1)
    parity = spread_row // (2 * n_chan)
    spread = ((spread_row - parity * 2 * n_chan) == spread_chan * 2 + parity).astype(jnp.bfloat16)
    for load in loads[:5]:
        load.wait()
    across = jnp.broadcast_to(owner_ref[...], (slots, slots))
    down = jnp.sum(jnp.where(here == there, across, 0), axis=1, keepdims=True)
    rank = jnp.sum(jnp.where((down == across) & (here < there), 1, 0), axis=0, keepdims=True)
    target = rank * n_devices + owner_ref[...]
    place = slot == target
    code = jnp.where(place, (column_ref[...] + 1).astype(jnp.float32), 0.0)
    code = jnp.broadcast_to(jnp.sum(code, axis=1, keepdims=True), (CAP * n_devices, LANES))
    for c in range(CAP):
        wide[pl.ds(base + CAP * tile_rows + c, n_devices, stride=rows), :] = code[
            c * n_devices : (c + 1) * n_devices
        ]
    x = x_ref[...].astype(jnp.float32)
    normed = []
    for t in range(lines):
        normed.append(standardize(x[:, t, :]).astype(jnp.bfloat16))
        right = dot_nt(second_ref[...], normed[t])
        groups = n_chan // right_rows
        packed = jnp.concatenate(
            [right[b * right_rows : (b + 1) * right_rows] for b in range(groups)], axis=1
        )
        for d in range(n_devices):
            wide[pl.ds(d * rows + t * right_rows, right_rows), :] = packed
    place = place.astype(jnp.bfloat16)
    for q in range(tile_rows):
        placed = dot(place, tiles_ref[:, q * LANES : (q + 1) * LANES])
        for c in range(CAP):
            wide[pl.ds(base + c * tile_rows + q, n_devices, stride=rows), :] = placed[
                c * n_devices : (c + 1) * n_devices
            ]
    send_ref[...] = wide[...].astype(jnp.bfloat16)

    for load in loads[5:7]:
        load.wait()
    first = dot(spread, first_ref[...]).astype(jnp.bfloat16)
    for t in range(lines):
        left = dot_nt(normed[t], first).astype(jnp.bfloat16).astype(jnp.float32)
        left_ref[pl.ds(t * depth, depth), :] = (left * (1.0 / depth)).astype(jnp.bfloat16)
    per_row = tile_rows // lines
    packed = tc // per_row
    row = lax.broadcasted_iota(jnp.int32, same_ref.shape, 0)
    lane = lax.broadcasted_iota(jnp.int32, same_ref.shape, 1)
    column = (row // tile_rows) * tc + (row % per_row) * packed + lane // (LANES // packed)
    line = lax.axis_index("row") * lines + (row % tile_rows) // per_row
    end = jnp.int32(0)
    column_chain = jnp.zeros_like(column)
    line_chain = jnp.zeros_like(line)
    for c in range(lengths_ref.shape[0]):
        end = end + lengths_ref[c]
        column_chain = column_chain + (column >= end).astype(jnp.int32)
        line_chain = line_chain + (line >= end).astype(jnp.int32)
    same_ref[...] = (column_chain == line_chain).astype(jnp.float32)
    for load in loads[7:]:
        load.wait()


def pair_kernel(
    n_devices,
    rows,
    tc,
    got_ref,
    left_ref,
    same_ref,
    tensor_ref,
    offset_ref,
    structural_ref,
    sigmoid_ref,
    content_ref,
    out_ref,
    folded,
    wide,
    sums,
    pair,
    opm,
):
    n_temp, pair_chan = structural_ref.shape
    lines = folded.shape[1] // pair_chan
    right_rows = folded.shape[0] // LANES
    depth = left_ref.shape[0] // lines
    n_tokens = n_devices * lines
    n_tiles = n_tokens // tc
    tile_rows = same_ref.shape[0] // n_tiles
    base = lines * right_rows

    width = left_ref.shape[1] // 2
    for p in range(tensor_ref.shape[0] // width):
        for parity in range(2):
            part = dot(
                left_ref[:, parity * width : (parity + 1) * width], tensor_ref[pl.ds(p * width, width), :]
            ).astype(jnp.bfloat16)
            d = 2 * p + parity
            at = (d % right_rows) * LANES + (d // right_rows) * depth
            for t in range(lines):
                folded[pl.ds(at, depth), t * pair_chan : (t + 1) * pair_chan] = part[t * depth : (t + 1) * depth]

    wide[...] = got_ref[...].astype(jnp.float32)

    unrolled = n_devices <= 16
    if not unrolled:
        sums[...] = jnp.zeros_like(sums)

    def add_source(d, carry):
        start = d * rows
        counts, totals = carry
        for c in range(CAP):
            tile = wide[pl.ds(start + base + c * tile_rows, tile_rows), :]
            code = wide[pl.ds(start + base + CAP * tile_rows + c, 1), :]
            for k in range(n_tiles):
                hit = code == k + 1.0
                counts[k] = counts[k] + jnp.where(hit, 1.0, 0.0)
                term = jnp.where(hit, tile, 0.0)
                if unrolled:
                    totals[k] = term if totals[k] is None else totals[k] + term
                else:
                    at = pl.ds(k * tile_rows, tile_rows)
                    sums[at, :] = sums[at, :] + term
        return counts, totals

    counts = [jnp.zeros((1, LANES), jnp.float32) for _ in range(n_tiles)]
    totals = [None] * n_tiles
    if unrolled:
        for d in range(n_devices):
            counts, totals = add_source(d, (counts, totals))
    else:
        counts = lax.fori_loop(0, n_devices, lambda d, kept: add_source(d, (kept, totals))[0], counts)
        totals = [sums[pl.ds(k * tile_rows, tile_rows), :] for k in range(n_tiles)]
    outer = None
    for g in range(right_rows):
        lhs = jnp.concatenate(
            [wide[pl.ds(t * right_rows + g, n_devices, stride=rows), :] for t in range(lines)], axis=0
        ).astype(jnp.bfloat16)
        term = dot(lhs, folded[pl.ds(g * LANES, LANES), :])
        outer = term if outer is None else outer + term
    order = exchange_order(n_devices)
    for i in range(lines):
        for t in range(lines):
            store_rows(
                opm,
                [i * n_tokens + d * lines + t for d in order],
                outer[t * n_devices : (t + 1) * n_devices, i * pair_chan : (i + 1) * pair_chan],
            )
    packed = LANES // n_temp
    per_row = tile_rows // lines
    for k in range(n_tiles):
        at = pl.ds(k * tile_rows, tile_rows)
        mean = totals[k] / jnp.maximum(counts[k], 1.0)
        template = (mean * same_ref[at, :]).astype(jnp.bfloat16)
        for h in range(packed):
            part = dot(template[:, h * n_temp : (h + 1) * n_temp], structural_ref[...])
            for i in range(lines):
                first = i * n_tokens + k * tc + h
                pair[pl.ds(first, per_row, stride=packed), :] = part[i * per_row : (i + 1) * per_row]
    for i in range(lines):
        at = pl.ds(i * n_tokens, n_tokens)
        total = pair[at, :] + (opm[at, :] + offset_ref[...].astype(jnp.float32))
        pair_normed = standardize(total).astype(jnp.bfloat16)
        gate = jax.nn.sigmoid(dot(pair_normed, sigmoid_ref[...]))
        linear = dot(pair_normed, content_ref[...])
        out_ref[at, :] = (gate * linear).astype(out_ref.dtype)


def grant(*arrays):
    return pltpu.CompilerParams(
        vmem_limit_bytes=sum(2 * math.prod(shape) * jnp.dtype(kind).itemsize for shape, kind in arrays) + (1 << 20)
    )


def on_device(
    aligned_sequences,
    first_factor_matrix,
    second_factor_matrix,
    tensor_matrix,
    tensor_offset,
    structural_duplex_patches,
    patch_source_index,
    patch_target_index,
    structural_matrix,
    polymer_residue_lengths,
    sigmoid_matrix,
    content_matrix,
):
    n_devices = lax.axis_size("row")
    depth, lines, n_feat = aligned_sequences.shape
    slots, width = structural_duplex_patches.shape
    n_chan = first_factor_matrix.shape[1]
    n_temp, pair_chan = structural_matrix.shape
    tc = width // (lines * n_temp)
    n_tokens = lines * n_devices
    n_tiles = n_tokens // tc
    tile_rows = width // LANES
    right_rows = n_chan * depth // LANES
    rows = lines * right_rows + CAP * tile_rows + CAP
    vmem = pl.BlockSpec(memory_space=VMEM)
    hbm = pl.BlockSpec(memory_space=HBM)
    half = n_chan // 2
    f32, bf16, i32 = jnp.float32, jnp.bfloat16, jnp.int32

    arguments = (
        aligned_sequences,
        second_factor_matrix.T,
        structural_duplex_patches,
        patch_source_index.reshape(1, slots),
        patch_target_index.reshape(1, slots),
        first_factor_matrix.T,
        polymer_residue_lengths,
        tensor_matrix.reshape(n_chan, half, 2, pair_chan),
        tensor_offset.reshape(1, pair_chan),
        structural_matrix,
        sigmoid_matrix,
        content_matrix,
    )
    results = (
        ((n_devices * rows, LANES), bf16),
        ((lines * depth, 4 * n_chan), bf16),
        ((n_tiles * tile_rows, LANES), f32),
        ((half, n_chan, 2, pair_chan), bf16),
        ((1, pair_chan), bf16),
        (structural_matrix.shape, bf16),
        (sigmoid_matrix.shape, bf16),
        (content_matrix.shape, bf16),
    )
    scratch = (
        (aligned_sequences.shape, bf16),
        ((n_chan, n_feat), bf16),
        ((slots, width), bf16),
        ((1, slots), i32),
        ((1, slots), i32),
        ((n_chan, n_feat), bf16),
    )
    packed_wide = ((n_devices * rows, LANES), f32)
    n_loads = 11 + half
    send, left, same, tensor, offset, structural, sigmoid, content = pl.pallas_call(
        functools.partial(pack_kernel, n_devices, rows, tc, n_loads),
        out_shape=[jax.ShapeDtypeStruct(*r) for r in results],
        in_specs=[hbm] * len(arguments),
        out_specs=[vmem] * len(results),
        scratch_shapes=[pltpu.VMEM(*a) for a in scratch]
        + [pltpu.SMEM(polymer_residue_lengths.shape, i32), pltpu.VMEM(*packed_wide)]
        + [pltpu.SemaphoreType.DMA((n_loads,))],
        compiler_params=grant(*results, *scratch, packed_wide),
    )(*(pltpu.with_memory_space_constraint(a, HBM) for a in arguments))
    got = lax.all_to_all(
        send.reshape(n_devices, rows // 2, 2, LANES),
        "row",
        split_axis=0,
        concat_axis=0,
        tiled=True,
        axis_index_groups=[exchange_order(n_devices)],
    ).reshape(n_devices * rows, LANES)
    tensor = tensor.reshape(n_chan * n_chan, pair_chan)
    scratch = (
        ((n_chan * depth, lines * pair_chan), bf16),
        packed_wide,
        ((n_tiles * tile_rows, LANES), f32),
        ((lines * n_tokens, pair_chan), f32),
        ((lines * n_tokens, pair_chan), f32),
    )
    result = ((lines * n_tokens, pair_chan), bf16)
    out = pl.pallas_call(
        functools.partial(pair_kernel, n_devices, rows, tc),
        out_shape=jax.ShapeDtypeStruct(*result),
        in_specs=[vmem] * 8,
        out_specs=vmem,
        scratch_shapes=[pltpu.VMEM(*a) for a in scratch],
        compiler_params=grant(*results, *scratch, result),
    )(got, left, same, tensor, offset, structural, sigmoid, content)
    return out.reshape(lines, n_tokens, pair_chan)


def solution(mesh):
    placed = (
        P(None, ("grp", "row"), None),
        P(),
        P(),
        P(),
        P(),
        P(("grp", "row"), None),
        P(("grp", "row"), None),
        P(("grp", "row")),
        P(),
        P("grp"),
        P(),
        P(),
    )
    return jax.shard_map(
        on_device,
        mesh=mesh,
        in_specs=placed,
        out_specs=P(("grp", "row"), None, None),
        check_vma=False,
    )
```

```python
import functools
import math

import jax
import jax.numpy as jnp
from jax import lax
from jax.experimental import pallas as pl
from jax.experimental.pallas import tpu as pltpu
from jax.sharding import PartitionSpec as P

CAP = 2
LANES = 128
ORDERS = {16: (8, 3, 5, 2, 15, 7, 12, 4, 14, 13, 10, 1, 6, 11, 0, 9)}
VMEM = pltpu.MemorySpace.VMEM
HBM = pltpu.MemorySpace.HBM


def dot(a, b):
    return jnp.dot(a, b, preferred_element_type=jnp.float32)


def dot_nt(a, b):
    return lax.dot_general(a, b, (((1,), (1,)), ((), ())), preferred_element_type=jnp.float32)


def exchange_order(n_devices):
    return ORDERS.get(n_devices, tuple(range(n_devices)))


def standardize(x):
    centred = x - jnp.mean(x, axis=-1, keepdims=True)
    variance = jnp.mean(centred * centred, axis=-1, keepdims=True)
    return centred * lax.rsqrt(variance + 1e-05)


def pack_kernel(n_devices, lines, rows, tc, *refs):
    (
        x_hbm,
        second_hbm,
        tiles_hbm,
        owner_hbm,
        column_hbm,
        first_hbm,
        lengths_hbm,
        tensor_hbm,
        offset_hbm,
        structural_hbm,
        sigmoid_hbm,
        content_hbm,
        send_ref,
        left_ref,
        same_ref,
        tensor_ref,
        offset_ref,
        weights_ref,
        features_ref,
        tiles_ref,
        index_ref,
        lengths_ref,
        normed_ref,
        wide,
        arrived,
    ) = refs

    def load(n, target, *sources):
        at = 0
        for source in sources:
            size = source.shape[0]
            pltpu.make_async_copy(source, target.at[pl.ds(at, size)], arrived.at[n]).start()
            at = at + size
        return pltpu.make_async_copy(target, target, arrived.at[n])

    index_load = load(0, index_ref, owner_hbm, column_hbm)
    features_load = load(1, features_ref, x_hbm, second_hbm, first_hbm)
    tiles_load = load(2, tiles_ref, tiles_hbm)
    lengths_load = pltpu.make_async_copy(lengths_hbm, lengths_ref, arrived.at[3])
    lengths_load.start()
    offset_load = load(4, offset_ref, offset_hbm)
    weights_load = load(5, weights_ref, structural_hbm, sigmoid_hbm, content_hbm)
    for p in range(tensor_ref.shape[0]):
        pltpu.make_async_copy(tensor_hbm.at[:, p], tensor_ref.at[p], arrived.at[6]).start()
    tensor_load = pltpu.make_async_copy(tensor_ref, tensor_ref, arrived.at[6])
    slots, width = tiles_ref.shape
    depth = left_ref.shape[0] // (2 * lines)
    tile_rows = width // LANES
    n_chan = second_hbm.shape[0]
    right_rows = n_chan * depth // LANES
    base = lines * right_rows
    per_row = tile_rows // lines
    packed = tc // per_row
    row = lax.broadcasted_iota(jnp.int32, same_ref.shape, 0)
    lane = lax.broadcasted_iota(jnp.int32, same_ref.shape, 1)
    column = (row // tile_rows) * tc + (row % per_row) * packed + lane // (LANES // packed)
    line = (row % tile_rows) // per_row
    here = lax.broadcasted_iota(jnp.int32, (slots, slots), 0)
    there = lax.broadcasted_iota(jnp.int32, (slots, slots), 1)
    order = exchange_order(n_devices)
    slot = lax.broadcasted_iota(jnp.int32, (CAP * n_devices, slots), 0)
    if order != tuple(range(n_devices)):
        position = slot % n_devices
        device = jnp.zeros_like(slot)
        for p, d in enumerate(order):
            device = jnp.where(position == p, d, device)
        slot = slot - position + device
    spread_row = lax.broadcasted_iota(jnp.int32, (4 * n_chan, n_chan), 0)
    spread_chan = lax.broadcasted_iota(jnp.int32, (4 * n_chan, n_chan), 1)
    parity = spread_row // (2 * n_chan)
    spread = ((spread_row - parity * 2 * n_chan) == spread_chan * 2 + parity).astype(jnp.bfloat16)
    index_load.wait()
    features_load.wait()
    lengths_load.wait()
    tiles_load.wait()
    owner = index_ref[pl.ds(0, 1), :]
    across = jnp.broadcast_to(owner, (slots, slots))
    down = jnp.sum(jnp.where(here == there, across, 0), axis=1, keepdims=True)
    rank = jnp.sum(jnp.where((down == across) & (here < there), 1, 0), axis=0, keepdims=True)
    target = rank * n_devices + owner
    place = slot == target
    code = jnp.where(place, (index_ref[pl.ds(1, 1), :] + 1).astype(jnp.float32), 0.0)
    code = jnp.broadcast_to(jnp.sum(code, axis=1, keepdims=True), (CAP * n_devices, LANES))
    for c in range(CAP):
        wide[pl.ds(base + CAP * tile_rows + c, n_devices, stride=rows), :] = code[
            c * n_devices : (c + 1) * n_devices
        ]
    height = lines * depth
    normed_ref[...] = standardize(features_ref[pl.ds(0, height), :].astype(jnp.float32))
    second = features_ref[pl.ds(height, n_chan), :]
    first = dot(spread, features_ref[pl.ds(height + n_chan, n_chan), :]).astype(jnp.bfloat16)
    groups = n_chan // right_rows
    for t in range(lines):
        normed = normed_ref[pl.ds(t, depth, stride=lines), :].astype(jnp.bfloat16)
        right = dot_nt(second, normed)
        right = jnp.concatenate(
            [right[b * right_rows : (b + 1) * right_rows] for b in range(groups)], axis=1
        )
        for d in range(n_devices):
            wide[pl.ds(d * rows + t * right_rows, right_rows), :] = right
        for parity in range(2):
            left = dot_nt(normed, first[parity * 2 * n_chan : (parity + 1) * 2 * n_chan])
            left = left.astype(jnp.bfloat16).astype(jnp.float32) * (1.0 / depth)
            left_ref[pl.ds((parity * lines + t) * depth, depth), :] = left.astype(jnp.bfloat16)
    place = place.astype(jnp.bfloat16)
    for q in range(tile_rows):
        placed = dot(place, tiles_ref[:, q * LANES : (q + 1) * LANES])
        for c in range(CAP):
            wide[pl.ds(base + c * tile_rows + q, n_devices, stride=rows), :] = placed[
                c * n_devices : (c + 1) * n_devices
            ]
    low = jnp.zeros_like(column)
    high = jnp.zeros_like(column)
    for i in range(lines):
        token = lax.axis_index("row") * lines + i
        end, below, above = jnp.int32(0), jnp.int32(0), jnp.int32(2**31 - 1)
        for c in range(lengths_ref.shape[0]):
            end = end + lengths_ref[c]
            below = jnp.where(end <= token, jnp.maximum(below, end), below)
            above = jnp.where(end <= token, above, jnp.minimum(above, end))
        low = jnp.where(line == i, below, low)
        high = jnp.where(line == i, above, high)
    same_ref[...] = ((column >= low) & (column < high)).astype(jnp.float32)
    send_ref[...] = wide[...].astype(jnp.bfloat16)
    offset_load.wait()
    weights_load.wait()
    tensor_load.wait()


def pair_kernel(
    n_devices,
    rows,
    tc,
    got_ref,
    left_ref,
    same_ref,
    tensor_ref,
    offset_ref,
    weights_ref,
    out_ref,
    folded,
    wide,
    sums,
    pair,
    opm,
):
    pair_chan = weights_ref.shape[1]
    n_temp = weights_ref.shape[0] - 2 * pair_chan
    structural = weights_ref[pl.ds(0, n_temp), :]
    sigmoid = weights_ref[pl.ds(n_temp, pair_chan), :]
    content = weights_ref[pl.ds(n_temp + pair_chan, pair_chan), :]
    lines = folded.shape[1] // pair_chan
    right_rows = folded.shape[0] // LANES
    depth = left_ref.shape[0] // (2 * lines)
    n_tokens = n_devices * lines
    n_tiles = n_tokens // tc
    tile_rows = same_ref.shape[0] // n_tiles
    base = lines * right_rows

    width = left_ref.shape[1]
    for p in range(0, tensor_ref.shape[0] // width, 2):
        both = jnp.concatenate(
            [tensor_ref[pl.ds(p * width, width), :], tensor_ref[pl.ds((p + 1) * width, width), :]], axis=1
        )
        part = dot(left_ref[...], both).astype(jnp.bfloat16)
        for n in range(2):
            for parity in range(2):
                d = 2 * (p + n) + parity
                at = (d % right_rows) * LANES + (d // right_rows) * depth
                for t in range(lines):
                    first = (parity * lines + t) * depth
                    folded[pl.ds(at, depth), t * pair_chan : (t + 1) * pair_chan] = part[
                        first : first + depth, n * pair_chan : (n + 1) * pair_chan
                    ]

    wide[...] = got_ref[...].astype(jnp.float32)
    few = min(n_devices, 16)
    slots = few * CAP
    span = slots * tile_rows
    kept = n_tiles * tile_rows
    slot_of = lax.broadcasted_iota(jnp.int32, (slots, span), 1) // tile_rows
    slot_is = lax.broadcasted_iota(jnp.int32, (slots, span), 0) == slot_of
    row_of = lax.broadcasted_iota(jnp.int32, (kept, span), 1) % tile_rows
    row = lax.broadcasted_iota(jnp.int32, (kept, span), 0)
    row_is = row % tile_rows == row_of
    wanted = (row // tile_rows + 1).astype(jnp.float32)

    def add_sources(first):
        codes = jnp.concatenate(
            [wide[pl.ds(first * rows + base + CAP * tile_rows + c, few, stride=rows), :] for c in range(CAP)], axis=0
        )
        across = jnp.concatenate([codes] * (span // LANES), axis=1)
        across = jnp.sum(jnp.where(slot_is, across, 0.0), axis=0, keepdims=True)
        landing = jnp.where(row_is & (across == wanted), 1.0, 0.0).astype(jnp.bfloat16)
        tiles = [
            wide[pl.ds((first + q) * rows + base + c * tile_rows, tile_rows), :].astype(jnp.bfloat16)
            for c in range(CAP)
            for q in range(few)
        ]
        counts = [
            jnp.sum(jnp.where(codes == k + 1.0, 1.0, 0.0), axis=0, keepdims=True) for k in range(n_tiles)
        ]
        return dot(landing, jnp.concatenate(tiles, axis=0)), counts

    total, counts = add_sources(0)
    if few < n_devices:
        sums[...] = total

        def add_more(n, counts):
            total, more = add_sources(n * few)
            sums[...] = sums[...] + total
            return tuple(a + b for a, b in zip(counts, more))

        counts = lax.fori_loop(1, n_devices // few, add_more, tuple(counts))
        total = sums[...]
    lhs = jnp.concatenate(
        [
            jnp.concatenate(
                [wide[pl.ds(t * right_rows + g, n_devices, stride=rows), :] for t in range(lines)], axis=0
            ).astype(jnp.bfloat16)
            for g in range(right_rows)
        ],
        axis=1,
    )
    outer = dot(lhs, folded[...])
    order = exchange_order(n_devices)
    for i in range(lines):
        for t in range(lines):
            part = outer[t * n_devices : (t + 1) * n_devices, i * pair_chan : (i + 1) * pair_chan]
            if order == tuple(range(n_devices)):
                opm[pl.ds(i * n_tokens + t, n_devices, stride=lines), :] = part
            else:
                for q, d in enumerate(order):
                    opm[pl.ds(i * n_tokens + d * lines + t, 1), :] = part[q : q + 1]
    packed = LANES // n_temp
    per_row = tile_rows // lines
    for k in range(n_tiles):
        at = pl.ds(k * tile_rows, tile_rows)
        mean = total[k * tile_rows : (k + 1) * tile_rows] / jnp.maximum(counts[k], 1.0)
        template = (mean * same_ref[at, :]).astype(jnp.bfloat16)
        for h in range(packed):
            part = dot(template[:, h * n_temp : (h + 1) * n_temp], structural)
            for i in range(lines):
                first = i * n_tokens + k * tc + h
                pair[pl.ds(first, per_row, stride=packed), :] = part[i * per_row : (i + 1) * per_row]
    for i in range(lines):
        at = pl.ds(i * n_tokens, n_tokens)
        total = pair[at, :] + (opm[at, :] + offset_ref[...].astype(jnp.float32))
        pair_normed = standardize(total).astype(jnp.bfloat16)
        gate = jax.nn.sigmoid(dot(pair_normed, sigmoid))
        linear = dot(pair_normed, content)
        out_ref[at, :] = (gate * linear).astype(out_ref.dtype)


def grant(*arrays):
    return pltpu.CompilerParams(
        vmem_limit_bytes=sum(2 * math.prod(shape) * jnp.dtype(kind).itemsize for shape, kind in arrays) + (1 << 20)
    )


def on_device(
    aligned_sequences,
    first_factor_matrix,
    second_factor_matrix,
    tensor_matrix,
    tensor_offset,
    structural_duplex_patches,
    patch_source_index,
    patch_target_index,
    structural_matrix,
    polymer_residue_lengths,
    sigmoid_matrix,
    content_matrix,
):
    n_devices = lax.axis_size("row")
    depth, lines, n_feat = aligned_sequences.shape
    slots, width = structural_duplex_patches.shape
    n_chan = first_factor_matrix.shape[1]
    n_temp, pair_chan = structural_matrix.shape
    tc = width // (lines * n_temp)
    n_tokens = lines * n_devices
    n_tiles = n_tokens // tc
    tile_rows = width // LANES
    right_rows = n_chan * depth // LANES
    rows = lines * right_rows + CAP * tile_rows + CAP
    vmem = pl.BlockSpec(memory_space=VMEM)
    hbm = pl.BlockSpec(memory_space=HBM)
    half = n_chan // 2
    f32, bf16, i32 = jnp.float32, jnp.bfloat16, jnp.int32

    arguments = (
        aligned_sequences.reshape(depth * lines, n_feat),
        second_factor_matrix.T,
        structural_duplex_patches,
        patch_source_index.reshape(1, slots),
        patch_target_index.reshape(1, slots),
        first_factor_matrix.T,
        polymer_residue_lengths,
        tensor_matrix.reshape(n_chan, half, 2, pair_chan),
        tensor_offset.reshape(1, pair_chan),
        structural_matrix,
        sigmoid_matrix,
        content_matrix,
    )
    results = (
        ((n_devices * rows, LANES), bf16),
        ((2 * lines * depth, 2 * n_chan), bf16),
        ((n_tiles * tile_rows, LANES), f32),
        ((half, n_chan, 2, pair_chan), bf16),
        ((1, pair_chan), bf16),
        ((n_temp + 2 * pair_chan, pair_chan), bf16),
    )
    scratch = (
        ((depth * lines + 2 * n_chan, n_feat), bf16),
        ((slots, width), bf16),
        ((2, slots), i32),
    )
    packed_wide = ((n_devices * rows, LANES), f32)
    send, left, same, tensor, offset, weights = pl.pallas_call(
        functools.partial(pack_kernel, n_devices, lines, rows, tc),
        out_shape=[jax.ShapeDtypeStruct(*r) for r in results],
        in_specs=[hbm] * len(arguments),
        out_specs=[vmem] * len(results),
        scratch_shapes=[pltpu.VMEM(*a) for a in scratch]
        + [pltpu.SMEM(polymer_residue_lengths.shape, i32), pltpu.VMEM((depth * lines, n_feat), f32)]
        + [pltpu.VMEM(*packed_wide)]
        + [pltpu.SemaphoreType.DMA((7,))],
        compiler_params=grant(*results, *scratch, packed_wide),
    )(*(pltpu.with_memory_space_constraint(a, HBM) for a in arguments))
    got = lax.all_to_all(
        send.reshape(n_devices, rows // 2, 2, LANES),
        "row",
        split_axis=0,
        concat_axis=0,
        tiled=True,
        axis_index_groups=[exchange_order(n_devices)],
    ).reshape(n_devices * rows, LANES)
    tensor = tensor.reshape(n_chan * n_chan, pair_chan)
    scratch = (
        ((n_chan * depth, lines * pair_chan), bf16),
        packed_wide,
        ((n_tiles * tile_rows, LANES), f32),
        ((lines * n_tokens, pair_chan), f32),
        ((lines * n_tokens, pair_chan), f32),
    )
    result = ((lines * n_tokens, pair_chan), bf16)
    out = pl.pallas_call(
        functools.partial(pair_kernel, n_devices, rows, tc),
        out_shape=jax.ShapeDtypeStruct(*result),
        in_specs=[vmem] * 6,
        out_specs=vmem,
        scratch_shapes=[pltpu.VMEM(*a) for a in scratch],
        compiler_params=grant(*results, *scratch, result),
    )(got, left, same, tensor, offset, weights)
    return out.reshape(lines, n_tokens, pair_chan)


def solution(mesh):
    placed = (
        P(None, ("grp", "row"), None),
        P(),
        P(),
        P(),
        P(),
        P(("grp", "row"), None),
        P(("grp", "row"), None),
        P(("grp", "row")),
        P(),
        P("grp"),
        P(),
        P(),
    )
    return jax.shard_map(
        on_device,
        mesh=mesh,
        in_specs=placed,
        out_specs=P(("grp", "row"), None, None),
        check_vma=False,
    )
```

```python
import functools
import math

import jax
import jax.numpy as jnp
from jax import lax
from jax.experimental import pallas as pl
from jax.experimental.pallas import tpu as pltpu
from jax.sharding import PartitionSpec as P

CAP = 2
LANES = 128
ORDERS = {16: (8, 3, 5, 2, 15, 7, 12, 4, 14, 13, 10, 1, 6, 11, 0, 9)}
VMEM = pltpu.MemorySpace.VMEM
HBM = pltpu.MemorySpace.HBM


def dot(a, b):
    return jnp.dot(a, b, preferred_element_type=jnp.float32)


def dot_nt(a, b):
    return lax.dot_general(a, b, (((1,), (1,)), ((), ())), preferred_element_type=jnp.float32)


def exchange_order(n_devices):
    return ORDERS.get(n_devices, tuple(range(n_devices)))


def standardize(x):
    centred = x - jnp.mean(x, axis=-1, keepdims=True)
    variance = jnp.mean(centred * centred, axis=-1, keepdims=True)
    return centred * lax.rsqrt(variance + 1e-05)


def pack_kernel(n_devices, lines, rows, tc, *refs):
    (
        x_hbm,
        second_hbm,
        tiles_hbm,
        owner_hbm,
        column_hbm,
        first_hbm,
        lengths_hbm,
        tensor_hbm,
        offset_hbm,
        structural_hbm,
        sigmoid_hbm,
        content_hbm,
        send_ref,
        left_ref,
        same_ref,
        tensor_ref,
        offset_ref,
        weights_ref,
        features_ref,
        tiles_ref,
        index_ref,
        lengths_ref,
        normed_ref,
        wide,
        arrived,
    ) = refs

    def load(n, target, *sources):
        at = 0
        for source in sources:
            size = source.shape[0]
            pltpu.make_async_copy(source, target.at[pl.ds(at, size)], arrived.at[n]).start()
            at = at + size
        return pltpu.make_async_copy(target, target, arrived.at[n])

    index_load = load(0, index_ref, owner_hbm, column_hbm)
    features_load = load(1, features_ref, x_hbm, second_hbm, first_hbm)
    tiles_load = load(2, tiles_ref, tiles_hbm)
    lengths_load = pltpu.make_async_copy(lengths_hbm, lengths_ref, arrived.at[3])
    lengths_load.start()
    offset_load = load(4, offset_ref, offset_hbm)
    weights_load = load(5, weights_ref, structural_hbm, sigmoid_hbm, content_hbm)
    for p in range(tensor_ref.shape[0]):
        pltpu.make_async_copy(tensor_hbm.at[:, p], tensor_ref.at[p], arrived.at[6]).start()
    tensor_load = pltpu.make_async_copy(tensor_ref, tensor_ref, arrived.at[6])
    slots, width = tiles_ref.shape
    depth = left_ref.shape[0] // (2 * lines)
    tile_rows = width // LANES
    n_chan = second_hbm.shape[0]
    right_rows = n_chan * depth // LANES
    base = lines * right_rows
    per_row = tile_rows // lines
    packed = tc // per_row
    row = lax.broadcasted_iota(jnp.int32, same_ref.shape, 0)
    lane = lax.broadcasted_iota(jnp.int32, same_ref.shape, 1)
    column = (row // tile_rows) * tc + (row % per_row) * packed + lane // (LANES // packed)
    line = (row % tile_rows) // per_row
    here = lax.broadcasted_iota(jnp.int32, (slots, slots), 0)
    there = lax.broadcasted_iota(jnp.int32, (slots, slots), 1)
    order = exchange_order(n_devices)
    slot = lax.broadcasted_iota(jnp.int32, (CAP * n_devices, slots), 0)
    if order != tuple(range(n_devices)):
        position = slot % n_devices
        device = jnp.zeros_like(slot)
        for p, d in enumerate(order):
            device = jnp.where(position == p, d, device)
        slot = slot - position + device
    spread_row = lax.broadcasted_iota(jnp.int32, (4 * n_chan, n_chan), 0)
    spread_chan = lax.broadcasted_iota(jnp.int32, (4 * n_chan, n_chan), 1)
    parity = spread_row // (2 * n_chan)
    spread = ((spread_row - parity * 2 * n_chan) == spread_chan * 2 + parity).astype(jnp.bfloat16)
    index_load.wait()
    features_load.wait()
    lengths_load.wait()
    tiles_load.wait()
    owner = index_ref[pl.ds(0, 1), :]
    across = jnp.broadcast_to(owner, (slots, slots))
    down = jnp.sum(jnp.where(here == there, across, 0), axis=1, keepdims=True)
    rank = jnp.sum(jnp.where((down == across) & (here < there), 1, 0), axis=0, keepdims=True)
    target = rank * n_devices + owner
    place = slot == target
    code = jnp.where(place, (index_ref[pl.ds(1, 1), :] + 1).astype(jnp.float32), 0.0)
    code = jnp.broadcast_to(jnp.sum(code, axis=1, keepdims=True), (CAP * n_devices, LANES))
    for c in range(CAP):
        wide[pl.ds(base + CAP * tile_rows + c, n_devices, stride=rows), :] = code[
            c * n_devices : (c + 1) * n_devices
        ]
    height = lines * depth
    normed_ref[...] = standardize(features_ref[pl.ds(0, height), :].astype(jnp.float32))
    second = features_ref[pl.ds(height, n_chan), :]
    first = dot(spread, features_ref[pl.ds(height + n_chan, n_chan), :]).astype(jnp.bfloat16)
    groups = n_chan // right_rows
    for t in range(lines):
        normed = normed_ref[pl.ds(t, depth, stride=lines), :].astype(jnp.bfloat16)
        right = dot_nt(second, normed)
        right = jnp.concatenate(
            [right[b * right_rows : (b + 1) * right_rows] for b in range(groups)], axis=1
        )
        for d in range(n_devices):
            wide[pl.ds(d * rows + t * right_rows, right_rows), :] = right
        for parity in range(2):
            left = dot_nt(normed, first[parity * 2 * n_chan : (parity + 1) * 2 * n_chan])
            left = left.astype(jnp.bfloat16).astype(jnp.float32) * (1.0 / depth)
            left_ref[pl.ds((parity * lines + t) * depth, depth), :] = left.astype(jnp.bfloat16)
    place = place.astype(jnp.bfloat16)
    for q in range(tile_rows):
        placed = dot(place, tiles_ref[:, q * LANES : (q + 1) * LANES])
        for c in range(CAP):
            wide[pl.ds(base + c * tile_rows + q, n_devices, stride=rows), :] = placed[
                c * n_devices : (c + 1) * n_devices
            ]
    low = jnp.zeros_like(column)
    high = jnp.zeros_like(column)
    for i in range(lines):
        token = lax.axis_index("row") * lines + i
        end, below, above = jnp.int32(0), jnp.int32(0), jnp.int32(2**31 - 1)
        for c in range(lengths_ref.shape[0]):
            end = end + lengths_ref[c]
            below = jnp.where(end <= token, jnp.maximum(below, end), below)
            above = jnp.where(end <= token, above, jnp.minimum(above, end))
        low = jnp.where(line == i, below, low)
        high = jnp.where(line == i, above, high)
    same_ref[...] = ((column >= low) & (column < high)).astype(jnp.float32)
    send_ref[...] = wide[...].astype(jnp.bfloat16)
    offset_load.wait()
    weights_load.wait()
    tensor_load.wait()


def pair_kernel(
    n_devices,
    rows,
    tc,
    got_ref,
    left_ref,
    same_ref,
    tensor_ref,
    offset_ref,
    weights_ref,
    out_ref,
    folded,
    wide,
    sums,
    pair,
):
    pair_chan = weights_ref.shape[1]
    n_temp = weights_ref.shape[0] - 2 * pair_chan
    structural = weights_ref[pl.ds(0, n_temp), :]
    sigmoid = weights_ref[pl.ds(n_temp, pair_chan), :]
    content = weights_ref[pl.ds(n_temp + pair_chan, pair_chan), :]
    lines = folded.shape[0]
    right_rows = folded.shape[1] // LANES
    depth = left_ref.shape[0] // (2 * lines)
    n_tokens = n_devices * lines
    n_tiles = n_tokens // tc
    tile_rows = same_ref.shape[0] // n_tiles
    base = lines * right_rows

    width = left_ref.shape[1]
    chans = tensor_ref.shape[0] // width
    half = right_rows // 2
    for p0 in range(half):
        for p in range(p0, chans, 2 * half):
            both = jnp.concatenate(
                [tensor_ref[pl.ds(p * width, width), :], tensor_ref[pl.ds((p + half) * width, width), :]], axis=1
            )
            part = dot(left_ref[...], both).astype(jnp.bfloat16)
            for n in range(2):
                for parity in range(2):
                    d = 2 * (p + n * half) + parity
                    at = (d % right_rows) * LANES + (d // right_rows) * depth
                    for t in range(lines):
                        first = (parity * lines + t) * depth
                        folded[t, pl.ds(at, depth), :] = part[
                            first : first + depth, n * pair_chan : (n + 1) * pair_chan
                        ]

    wide[...] = got_ref[...].astype(jnp.float32)
    few = min(n_devices, 16)
    slots = few * CAP
    span = slots * tile_rows
    kept = n_tiles * tile_rows
    slot_of = lax.broadcasted_iota(jnp.int32, (slots, span), 1) // tile_rows
    slot_is = lax.broadcasted_iota(jnp.int32, (slots, span), 0) == slot_of
    row_of = lax.broadcasted_iota(jnp.int32, (kept, span), 1) % tile_rows
    row = lax.broadcasted_iota(jnp.int32, (kept, span), 0)
    row_is = row % tile_rows == row_of
    wanted = (row // tile_rows + 1).astype(jnp.float32)

    def add_sources(first):
        codes = jnp.concatenate(
            [wide[pl.ds(first * rows + base + CAP * tile_rows + c, few, stride=rows), :] for c in range(CAP)], axis=0
        )
        across = jnp.concatenate([codes] * (span // LANES), axis=1)
        across = jnp.sum(jnp.where(slot_is, across, 0.0), axis=0, keepdims=True)
        landing = jnp.where(row_is & (across == wanted), 1.0, 0.0).astype(jnp.bfloat16)
        tiles = [
            wide[pl.ds((first + q) * rows + base + c * tile_rows, tile_rows), :].astype(jnp.bfloat16)
            for c in range(CAP)
            for q in range(few)
        ]
        counts = [
            jnp.sum(jnp.where(codes == k + 1.0, 1.0, 0.0), axis=0, keepdims=True) for k in range(n_tiles)
        ]
        return dot(landing, jnp.concatenate(tiles, axis=0)), counts

    total, counts = add_sources(0)
    if few < n_devices:
        sums[...] = total

        def add_more(n, counts):
            total, more = add_sources(n * few)
            sums[...] = sums[...] + total
            return tuple(a + b for a, b in zip(counts, more))

        counts = lax.fori_loop(1, n_devices // few, add_more, tuple(counts))
        total = sums[...]
    lhs = jnp.concatenate(
        [
            jnp.concatenate(
                [wide[pl.ds(t * right_rows + g, n_devices, stride=rows), :] for t in range(lines)], axis=0
            ).astype(jnp.bfloat16)
            for g in range(right_rows)
        ],
        axis=1,
    )
    order = exchange_order(n_devices)
    token = lax.broadcasted_iota(jnp.int32, (n_tokens, n_tokens), 0)
    held = lax.broadcasted_iota(jnp.int32, (n_tokens, n_tokens), 1)
    position = held % n_devices
    device = position
    if order != tuple(range(n_devices)):
        device = jnp.zeros_like(held)
        for p, d in enumerate(order):
            device = jnp.where(position == p, d, device)
    swap = (token == device * lines + held // n_devices).astype(jnp.bfloat16)
    lhs = dot(swap, lhs).astype(jnp.bfloat16)
    outer = None
    step = folded.shape[1] // 2
    for at in range(0, folded.shape[1], step):
        term = dot(
            lhs[:, at : at + step],
            jnp.concatenate([folded[i, pl.ds(at, step), :] for i in range(lines)], axis=1),
        )
        outer = term if outer is None else outer + term
    packed = LANES // n_temp
    per_row = tile_rows // lines
    for k in range(n_tiles):
        at = pl.ds(k * tile_rows, tile_rows)
        mean = total[k * tile_rows : (k + 1) * tile_rows] / jnp.maximum(counts[k], 1.0)
        template = (mean * same_ref[at, :]).astype(jnp.bfloat16)
        for h in range(packed):
            part = dot(template[:, h * n_temp : (h + 1) * n_temp], structural)
            for i in range(lines):
                first = i * n_tokens + k * tc + h
                pair[pl.ds(first, per_row, stride=packed), :] = part[i * per_row : (i + 1) * per_row]
    for i in range(lines):
        at = pl.ds(i * n_tokens, n_tokens)
        total = pair[at, :] + (
            outer[:, i * pair_chan : (i + 1) * pair_chan] + offset_ref[...].astype(jnp.float32)
        )
        pair_normed = standardize(total).astype(jnp.bfloat16)
        gate = jax.nn.sigmoid(dot(pair_normed, sigmoid))
        linear = dot(pair_normed, content)
        out_ref[at, :] = (gate * linear).astype(out_ref.dtype)


def grant(*arrays):
    return pltpu.CompilerParams(
        vmem_limit_bytes=sum(2 * math.prod(shape) * jnp.dtype(kind).itemsize for shape, kind in arrays) + (1 << 20)
    )


def on_device(
    aligned_sequences,
    first_factor_matrix,
    second_factor_matrix,
    tensor_matrix,
    tensor_offset,
    structural_duplex_patches,
    patch_source_index,
    patch_target_index,
    structural_matrix,
    polymer_residue_lengths,
    sigmoid_matrix,
    content_matrix,
):
    n_devices = lax.axis_size("row")
    depth, lines, n_feat = aligned_sequences.shape
    slots, width = structural_duplex_patches.shape
    n_chan = first_factor_matrix.shape[1]
    n_temp, pair_chan = structural_matrix.shape
    tc = width // (lines * n_temp)
    n_tokens = lines * n_devices
    n_tiles = n_tokens // tc
    tile_rows = width // LANES
    right_rows = n_chan * depth // LANES
    rows = lines * right_rows + CAP * tile_rows + CAP
    vmem = pl.BlockSpec(memory_space=VMEM)
    hbm = pl.BlockSpec(memory_space=HBM)
    half = n_chan // 2
    f32, bf16, i32 = jnp.float32, jnp.bfloat16, jnp.int32

    arguments = (
        aligned_sequences.reshape(depth * lines, n_feat),
        second_factor_matrix.T,
        structural_duplex_patches,
        patch_source_index.reshape(1, slots),
        patch_target_index.reshape(1, slots),
        first_factor_matrix.T,
        polymer_residue_lengths,
        tensor_matrix.reshape(n_chan, half, 2, pair_chan),
        tensor_offset.reshape(1, pair_chan),
        structural_matrix,
        sigmoid_matrix,
        content_matrix,
    )
    results = (
        ((n_devices * rows, LANES), bf16),
        ((2 * lines * depth, 2 * n_chan), bf16),
        ((n_tiles * tile_rows, LANES), f32),
        ((half, n_chan, 2, pair_chan), bf16),
        ((1, pair_chan), bf16),
        ((n_temp + 2 * pair_chan, pair_chan), bf16),
    )
    scratch = (
        ((depth * lines + 2 * n_chan, n_feat), bf16),
        ((slots, width), bf16),
        ((2, slots), i32),
    )
    packed_wide = ((n_devices * rows, LANES), f32)
    send, left, same, tensor, offset, weights = pl.pallas_call(
        functools.partial(pack_kernel, n_devices, lines, rows, tc),
        out_shape=[jax.ShapeDtypeStruct(*r) for r in results],
        in_specs=[hbm] * len(arguments),
        out_specs=[vmem] * len(results),
        scratch_shapes=[pltpu.VMEM(*a) for a in scratch]
        + [pltpu.SMEM(polymer_residue_lengths.shape, i32), pltpu.VMEM((depth * lines, n_feat), f32)]
        + [pltpu.VMEM(*packed_wide)]
        + [pltpu.SemaphoreType.DMA((7,))],
        compiler_params=grant(*results, *scratch, packed_wide),
    )(*(pltpu.with_memory_space_constraint(a, HBM) for a in arguments))
    got = lax.all_to_all(
        send.reshape(n_devices, rows // 2, 2, LANES),
        "row",
        split_axis=0,
        concat_axis=0,
        tiled=True,
        axis_index_groups=[exchange_order(n_devices)],
    ).reshape(n_devices * rows, LANES)
    tensor = tensor.reshape(n_chan * n_chan, pair_chan)
    scratch = (
        ((lines, n_chan * depth, pair_chan), bf16),
        packed_wide,
        ((n_tiles * tile_rows, LANES), f32),
        ((lines * n_tokens, pair_chan), f32),
    )
    result = ((lines * n_tokens, pair_chan), bf16)
    out = pl.pallas_call(
        functools.partial(pair_kernel, n_devices, rows, tc),
        out_shape=jax.ShapeDtypeStruct(*result),
        in_specs=[vmem] * 6,
        out_specs=vmem,
        scratch_shapes=[pltpu.VMEM(*a) for a in scratch],
        compiler_params=grant(*results, *scratch, result),
    )(got, left, same, tensor, offset, weights)
    return out.reshape(lines, n_tokens, pair_chan)


def solution(mesh):
    placed = (
        P(None, ("grp", "row"), None),
        P(),
        P(),
        P(),
        P(),
        P(("grp", "row"), None),
        P(("grp", "row"), None),
        P(("grp", "row")),
        P(),
        P("grp"),
        P(),
        P(),
    )
    return jax.shard_map(
        on_device,
        mesh=mesh,
        in_specs=placed,
        out_specs=P(("grp", "row"), None, None),
        check_vma=False,
    )
```

```python
import functools
import math

import jax
import jax.numpy as jnp
from jax import lax
from jax.experimental import pallas as pl
from jax.experimental.pallas import tpu as pltpu
from jax.sharding import PartitionSpec as P

CAP = 2
LANES = 128
ORDERS = {16: (11, 0, 9, 8, 15, 5, 3, 1, 7, 12, 4, 14, 13, 10, 2, 6)}
VMEM = pltpu.MemorySpace.VMEM
HBM = pltpu.MemorySpace.HBM


def dot(a, b):
    return jnp.dot(a, b, preferred_element_type=jnp.float32)


def dot_nt(a, b):
    return lax.dot_general(a, b, (((1,), (1,)), ((), ())), preferred_element_type=jnp.float32)


def exchange_order(n_devices):
    return ORDERS.get(n_devices, tuple(range(n_devices)))


def standardize(x):
    centred = x - jnp.mean(x, axis=-1, keepdims=True)
    variance = jnp.mean(centred * centred, axis=-1, keepdims=True)
    return centred * lax.rsqrt(variance + 1e-05)


def pack_kernel(n_devices, lines, rows, tc, *refs):
    (
        x_hbm,
        second_hbm,
        tiles_hbm,
        owner_hbm,
        column_hbm,
        first_hbm,
        lengths_hbm,
        tensor_hbm,
        offset_hbm,
        structural_hbm,
        sigmoid_hbm,
        content_hbm,
        send_ref,
        left_ref,
        same_ref,
        tensor_ref,
        offset_ref,
        weights_ref,
        features_ref,
        tiles_ref,
        index_ref,
        lengths_ref,
        normed_ref,
        wide,
        arrived,
    ) = refs

    def load(n, target, *sources):
        at = 0
        for source in sources:
            size = source.shape[0]
            pltpu.make_async_copy(source, target.at[pl.ds(at, size)], arrived.at[n]).start()
            at = at + size
        return pltpu.make_async_copy(target, target, arrived.at[n])

    index_load = load(0, index_ref, owner_hbm, column_hbm)
    features_load = load(1, features_ref, x_hbm, second_hbm, first_hbm)
    tiles_load = load(2, tiles_ref, tiles_hbm)
    lengths_load = pltpu.make_async_copy(lengths_hbm, lengths_ref, arrived.at[3])
    lengths_load.start()
    offset_load = load(4, offset_ref, offset_hbm)
    weights_load = load(5, weights_ref, structural_hbm, sigmoid_hbm, content_hbm)
    for p in range(tensor_ref.shape[0]):
        pltpu.make_async_copy(tensor_hbm.at[:, p], tensor_ref.at[p], arrived.at[6]).start()
    tensor_load = pltpu.make_async_copy(tensor_ref, tensor_ref, arrived.at[6])
    slots, width = tiles_ref.shape
    depth = left_ref.shape[0] // (2 * lines)
    tile_rows = width // LANES
    n_chan = second_hbm.shape[0]
    right_rows = n_chan * depth // LANES
    base = lines * right_rows
    per_row = tile_rows // lines
    packed = tc // per_row
    row = lax.broadcasted_iota(jnp.int32, same_ref.shape, 0)
    lane = lax.broadcasted_iota(jnp.int32, same_ref.shape, 1)
    column = (row // tile_rows) * tc + (row % per_row) * packed + lane // (LANES // packed)
    line = (row % tile_rows) // per_row
    here = lax.broadcasted_iota(jnp.int32, (slots, slots), 0)
    there = lax.broadcasted_iota(jnp.int32, (slots, slots), 1)
    order = exchange_order(n_devices)
    slot = lax.broadcasted_iota(jnp.int32, (CAP * n_devices, slots), 0)
    if order != tuple(range(n_devices)):
        position = slot % n_devices
        device = jnp.zeros_like(slot)
        for p, d in enumerate(order):
            device = jnp.where(position == p, d, device)
        slot = slot - position + device
    spread_row = lax.broadcasted_iota(jnp.int32, (4 * n_chan, n_chan), 0)
    spread_chan = lax.broadcasted_iota(jnp.int32, (4 * n_chan, n_chan), 1)
    parity = spread_row // (2 * n_chan)
    spread = ((spread_row - parity * 2 * n_chan) == spread_chan * 2 + parity).astype(jnp.bfloat16)
    index_load.wait()
    features_load.wait()
    lengths_load.wait()
    tiles_load.wait()
    owner = index_ref[pl.ds(0, 1), :]
    across = jnp.broadcast_to(owner, (slots, slots))
    down = jnp.sum(jnp.where(here == there, across, 0), axis=1, keepdims=True)
    rank = jnp.sum(jnp.where((down == across) & (here < there), 1, 0), axis=0, keepdims=True)
    target = rank * n_devices + owner
    place = slot == target
    code = jnp.where(place, (index_ref[pl.ds(1, 1), :] + 1).astype(jnp.float32), 0.0)
    code = jnp.broadcast_to(jnp.sum(code, axis=1, keepdims=True), (CAP * n_devices, LANES))
    for c in range(CAP):
        wide[pl.ds(base + CAP * tile_rows + c, n_devices, stride=rows), :] = code[
            c * n_devices : (c + 1) * n_devices
        ]
    height = lines * depth
    normed_ref[...] = standardize(features_ref[pl.ds(0, height), :].astype(jnp.float32))
    second = features_ref[pl.ds(height, n_chan), :]
    first = dot(spread, features_ref[pl.ds(height + n_chan, n_chan), :]).astype(jnp.bfloat16)
    groups = n_chan // right_rows
    for t in range(lines):
        normed = normed_ref[pl.ds(t, depth, stride=lines), :].astype(jnp.bfloat16)
        right = dot_nt(second, normed)
        right = jnp.concatenate(
            [right[b * right_rows : (b + 1) * right_rows] for b in range(groups)], axis=1
        )
        for d in range(n_devices):
            wide[pl.ds(d * rows + t * right_rows, right_rows), :] = right
        for parity in range(2):
            left = dot_nt(normed, first[parity * 2 * n_chan : (parity + 1) * 2 * n_chan])
            left = left.astype(jnp.bfloat16).astype(jnp.float32) * (1.0 / depth)
            left_ref[pl.ds((parity * lines + t) * depth, depth), :] = left.astype(jnp.bfloat16)
    place = place.astype(jnp.bfloat16)
    for q in range(tile_rows):
        placed = dot(place, tiles_ref[:, q * LANES : (q + 1) * LANES])
        for c in range(CAP):
            wide[pl.ds(base + c * tile_rows + q, n_devices, stride=rows), :] = placed[
                c * n_devices : (c + 1) * n_devices
            ]
    low = jnp.zeros_like(column)
    high = jnp.zeros_like(column)
    for i in range(lines):
        token = lax.axis_index("row") * lines + i
        end, below, above = jnp.int32(0), jnp.int32(0), jnp.int32(2**31 - 1)
        for c in range(lengths_ref.shape[0]):
            end = end + lengths_ref[c]
            below = jnp.where(end <= token, jnp.maximum(below, end), below)
            above = jnp.where(end <= token, above, jnp.minimum(above, end))
        low = jnp.where(line == i, below, low)
        high = jnp.where(line == i, above, high)
    same_ref[...] = ((column >= low) & (column < high)).astype(jnp.float32)
    send_ref[...] = wide[...].astype(jnp.bfloat16)
    offset_load.wait()
    weights_load.wait()
    tensor_load.wait()


def pair_kernel(
    n_devices,
    rows,
    tc,
    got_ref,
    left_ref,
    same_ref,
    tensor_ref,
    offset_ref,
    weights_ref,
    out_ref,
    folded,
    wide,
    sums,
    pair,
):
    pair_chan = weights_ref.shape[1]
    n_temp = weights_ref.shape[0] - 2 * pair_chan
    structural = weights_ref[pl.ds(0, n_temp), :]
    sigmoid = weights_ref[pl.ds(n_temp, pair_chan), :]
    content = weights_ref[pl.ds(n_temp + pair_chan, pair_chan), :]
    lines = folded.shape[0]
    right_rows = folded.shape[1] // LANES
    depth = left_ref.shape[0] // (2 * lines)
    n_tokens = n_devices * lines
    n_tiles = n_tokens // tc
    tile_rows = same_ref.shape[0] // n_tiles
    base = lines * right_rows

    width = left_ref.shape[1]
    chans = tensor_ref.shape[0] // width
    half = right_rows // 2
    for p0 in range(half):
        for p in range(p0, chans, 2 * half):
            both = jnp.concatenate(
                [tensor_ref[pl.ds(p * width, width), :], tensor_ref[pl.ds((p + half) * width, width), :]], axis=1
            )
            part = dot(left_ref[...], both).astype(jnp.bfloat16)
            for n in range(2):
                for parity in range(2):
                    d = 2 * (p + n * half) + parity
                    at = (d % right_rows) * LANES + (d // right_rows) * depth
                    for t in range(lines):
                        first = (parity * lines + t) * depth
                        folded[t, pl.ds(at, depth), :] = part[
                            first : first + depth, n * pair_chan : (n + 1) * pair_chan
                        ]

    wide[...] = got_ref[...].astype(jnp.float32)
    few = min(n_devices, 16)
    slots = few * CAP
    span = slots * tile_rows
    kept = n_tiles * tile_rows
    slot_of = lax.broadcasted_iota(jnp.int32, (slots, span), 1) // tile_rows
    slot_is = lax.broadcasted_iota(jnp.int32, (slots, span), 0) == slot_of
    row_of = lax.broadcasted_iota(jnp.int32, (kept, span), 1) % tile_rows
    row = lax.broadcasted_iota(jnp.int32, (kept, span), 0)
    row_is = row % tile_rows == row_of
    wanted = (row // tile_rows + 1).astype(jnp.float32)

    def add_sources(first):
        codes = jnp.concatenate(
            [wide[pl.ds(first * rows + base + CAP * tile_rows + c, few, stride=rows), :] for c in range(CAP)], axis=0
        )
        across = jnp.concatenate([codes] * (span // LANES), axis=1)
        across = jnp.sum(jnp.where(slot_is, across, 0.0), axis=0, keepdims=True)
        landing = jnp.where(row_is & (across == wanted), 1.0, 0.0).astype(jnp.bfloat16)
        tiles = [
            wide[pl.ds((first + q) * rows + base + c * tile_rows, tile_rows), :].astype(jnp.bfloat16)
            for c in range(CAP)
            for q in range(few)
        ]
        counts = [
            jnp.sum(jnp.where(codes == k + 1.0, 1.0, 0.0), axis=0, keepdims=True) for k in range(n_tiles)
        ]
        return dot(landing, jnp.concatenate(tiles, axis=0)), counts

    total, counts = add_sources(0)
    if few < n_devices:
        sums[...] = total

        def add_more(n, counts):
            total, more = add_sources(n * few)
            sums[...] = sums[...] + total
            return tuple(a + b for a, b in zip(counts, more))

        counts = lax.fori_loop(1, n_devices // few, add_more, tuple(counts))
        total = sums[...]
    lhs = jnp.concatenate(
        [
            jnp.concatenate(
                [wide[pl.ds(t * right_rows + g, n_devices, stride=rows), :] for t in range(lines)], axis=0
            ).astype(jnp.bfloat16)
            for g in range(right_rows)
        ],
        axis=1,
    )
    order = exchange_order(n_devices)
    token = lax.broadcasted_iota(jnp.int32, (n_tokens, n_tokens), 0)
    held = lax.broadcasted_iota(jnp.int32, (n_tokens, n_tokens), 1)
    position = held % n_devices
    device = position
    if order != tuple(range(n_devices)):
        device = jnp.zeros_like(held)
        for p, d in enumerate(order):
            device = jnp.where(position == p, d, device)
    swap = (token == device * lines + held // n_devices).astype(jnp.bfloat16)
    lhs = dot(swap, lhs).astype(jnp.bfloat16)
    outer = None
    step = folded.shape[1] // 2
    for at in range(0, folded.shape[1], step):
        term = dot(
            lhs[:, at : at + step],
            jnp.concatenate([folded[i, pl.ds(at, step), :] for i in range(lines)], axis=1),
        )
        outer = term if outer is None else outer + term
    packed = LANES // n_temp
    per_row = tile_rows // lines
    for k in range(n_tiles):
        at = pl.ds(k * tile_rows, tile_rows)
        mean = total[k * tile_rows : (k + 1) * tile_rows] / jnp.maximum(counts[k], 1.0)
        template = (mean * same_ref[at, :]).astype(jnp.bfloat16)
        for h in range(packed):
            part = dot(template[:, h * n_temp : (h + 1) * n_temp], structural)
            for i in range(lines):
                first = i * n_tokens + k * tc + h
                pair[pl.ds(first, per_row, stride=packed), :] = part[i * per_row : (i + 1) * per_row]
    for i in range(lines):
        at = pl.ds(i * n_tokens, n_tokens)
        total = pair[at, :] + (
            outer[:, i * pair_chan : (i + 1) * pair_chan] + offset_ref[...].astype(jnp.float32)
        )
        pair_normed = standardize(total).astype(jnp.bfloat16)
        gate = jax.nn.sigmoid(dot(pair_normed, sigmoid))
        linear = dot(pair_normed, content)
        out_ref[at, :] = (gate * linear).astype(out_ref.dtype)


def grant(*arrays):
    return pltpu.CompilerParams(
        vmem_limit_bytes=sum(2 * math.prod(shape) * jnp.dtype(kind).itemsize for shape, kind in arrays) + (1 << 20)
    )


def on_device(
    aligned_sequences,
    first_factor_matrix,
    second_factor_matrix,
    tensor_matrix,
    tensor_offset,
    structural_duplex_patches,
    patch_source_index,
    patch_target_index,
    structural_matrix,
    polymer_residue_lengths,
    sigmoid_matrix,
    content_matrix,
):
    n_devices = lax.axis_size("row")
    depth, lines, n_feat = aligned_sequences.shape
    slots, width = structural_duplex_patches.shape
    n_chan = first_factor_matrix.shape[1]
    n_temp, pair_chan = structural_matrix.shape
    tc = width // (lines * n_temp)
    n_tokens = lines * n_devices
    n_tiles = n_tokens // tc
    tile_rows = width // LANES
    right_rows = n_chan * depth // LANES
    rows = lines * right_rows + CAP * tile_rows + CAP
    vmem = pl.BlockSpec(memory_space=VMEM)
    hbm = pl.BlockSpec(memory_space=HBM)
    half = n_chan // 2
    f32, bf16, i32 = jnp.float32, jnp.bfloat16, jnp.int32

    arguments = (
        aligned_sequences.reshape(depth * lines, n_feat),
        second_factor_matrix.T,
        structural_duplex_patches,
        patch_source_index.reshape(1, slots),
        patch_target_index.reshape(1, slots),
        first_factor_matrix.T,
        polymer_residue_lengths,
        tensor_matrix.reshape(n_chan, half, 2, pair_chan),
        tensor_offset.reshape(1, pair_chan),
        structural_matrix,
        sigmoid_matrix,
        content_matrix,
    )
    results = (
        ((n_devices * rows, LANES), bf16),
        ((2 * lines * depth, 2 * n_chan), bf16),
        ((n_tiles * tile_rows, LANES), f32),
        ((half, n_chan, 2, pair_chan), bf16),
        ((1, pair_chan), bf16),
        ((n_temp + 2 * pair_chan, pair_chan), bf16),
    )
    scratch = (
        ((depth * lines + 2 * n_chan, n_feat), bf16),
        ((slots, width), bf16),
        ((2, slots), i32),
    )
    packed_wide = ((n_devices * rows, LANES), f32)
    send, left, same, tensor, offset, weights = pl.pallas_call(
        functools.partial(pack_kernel, n_devices, lines, rows, tc),
        out_shape=[jax.ShapeDtypeStruct(*r) for r in results],
        in_specs=[hbm] * len(arguments),
        out_specs=[vmem] * len(results),
        scratch_shapes=[pltpu.VMEM(*a) for a in scratch]
        + [pltpu.SMEM(polymer_residue_lengths.shape, i32), pltpu.VMEM((depth * lines, n_feat), f32)]
        + [pltpu.VMEM(*packed_wide)]
        + [pltpu.SemaphoreType.DMA((7,))],
        compiler_params=grant(*results, *scratch, packed_wide),
    )(*(pltpu.with_memory_space_constraint(a, HBM) for a in arguments))
    got = lax.all_to_all(
        send.reshape(n_devices, rows // 2, 2, LANES),
        "row",
        split_axis=0,
        concat_axis=0,
        tiled=True,
        axis_index_groups=[exchange_order(n_devices)],
    ).reshape(n_devices * rows, LANES)
    tensor = tensor.reshape(n_chan * n_chan, pair_chan)
    scratch = (
        ((lines, n_chan * depth, pair_chan), bf16),
        packed_wide,
        ((n_tiles * tile_rows, LANES), f32),
        ((lines * n_tokens, pair_chan), f32),
    )
    result = ((lines * n_tokens, pair_chan), bf16)
    out = pl.pallas_call(
        functools.partial(pair_kernel, n_devices, rows, tc),
        out_shape=jax.ShapeDtypeStruct(*result),
        in_specs=[vmem] * 6,
        out_specs=vmem,
        scratch_shapes=[pltpu.VMEM(*a) for a in scratch],
        compiler_params=grant(*results, *scratch, result),
    )(got, left, same, tensor, offset, weights)
    return out.reshape(lines, n_tokens, pair_chan)


def solution(mesh):
    placed = (
        P(None, ("grp", "row"), None),
        P(),
        P(),
        P(),
        P(),
        P(("grp", "row"), None),
        P(("grp", "row"), None),
        P(("grp", "row")),
        P(),
        P("grp"),
        P(),
        P(),
    )
    return jax.shard_map(
        on_device,
        mesh=mesh,
        in_specs=placed,
        out_specs=P(("grp", "row"), None, None),
        check_vma=False,
    )
```

```python
import functools
import math

import jax
import jax.numpy as jnp
from jax import lax
from jax.experimental import pallas as pl
from jax.experimental.pallas import tpu as pltpu
from jax.sharding import PartitionSpec as P

CAP = 2
LANES = 128
ORDERS = {16: (11, 0, 2, 8, 5, 7, 3, 1, 13, 14, 4, 12, 15, 10, 9, 6)}
VMEM = pltpu.MemorySpace.VMEM
HBM = pltpu.MemorySpace.HBM


def dot(a, b):
    return jnp.dot(a, b, preferred_element_type=jnp.float32)


def dot_nt(a, b):
    return lax.dot_general(a, b, (((1,), (1,)), ((), ())), preferred_element_type=jnp.float32)


def exchange_order(n_devices):
    return ORDERS.get(n_devices, tuple(range(n_devices)))


def standardize(x):
    centred = x - jnp.mean(x, axis=-1, keepdims=True)
    variance = jnp.mean(centred * centred, axis=-1, keepdims=True)
    return centred * lax.rsqrt(variance + 1e-05)


def pack_kernel(n_devices, lines, rows, tc, *refs):
    (
        x_hbm,
        second_hbm,
        tiles_hbm,
        owner_hbm,
        column_hbm,
        first_hbm,
        lengths_hbm,
        tensor_hbm,
        offset_hbm,
        structural_hbm,
        sigmoid_hbm,
        content_hbm,
        send_ref,
        left_ref,
        same_ref,
        tensor_ref,
        offset_ref,
        weights_ref,
        features_ref,
        tiles_ref,
        index_ref,
        lengths_ref,
        normed_ref,
        wide,
        arrived,
    ) = refs

    def load(n, target, *sources):
        at = 0
        for source in sources:
            size = source.shape[0]
            pltpu.make_async_copy(source, target.at[pl.ds(at, size)], arrived.at[n]).start()
            at = at + size
        return pltpu.make_async_copy(target, target, arrived.at[n])

    index_load = load(0, index_ref, owner_hbm, column_hbm)
    features_load = load(1, features_ref, x_hbm, second_hbm, first_hbm)
    tiles_load = load(2, tiles_ref, tiles_hbm)
    lengths_load = pltpu.make_async_copy(lengths_hbm, lengths_ref, arrived.at[3])
    lengths_load.start()
    offset_load = load(4, offset_ref, offset_hbm)
    weights_load = load(5, weights_ref, structural_hbm, sigmoid_hbm, content_hbm)
    for p in range(tensor_ref.shape[0]):
        pltpu.make_async_copy(tensor_hbm.at[:, p], tensor_ref.at[p], arrived.at[6]).start()
    tensor_load = pltpu.make_async_copy(tensor_ref, tensor_ref, arrived.at[6])
    slots, width = tiles_ref.shape
    depth = left_ref.shape[0] // (2 * lines)
    tile_rows = width // LANES
    n_chan = second_hbm.shape[0]
    right_rows = n_chan * depth // LANES
    base = lines * right_rows
    per_row = tile_rows // lines
    packed = tc // per_row
    row = lax.broadcasted_iota(jnp.int32, same_ref.shape, 0)
    lane = lax.broadcasted_iota(jnp.int32, same_ref.shape, 1)
    column = (row // tile_rows) * tc + (row % per_row) * packed + lane // (LANES // packed)
    line = (row % tile_rows) // per_row
    here = lax.broadcasted_iota(jnp.int32, (slots, slots), 0)
    there = lax.broadcasted_iota(jnp.int32, (slots, slots), 1)
    order = exchange_order(n_devices)
    slot = lax.broadcasted_iota(jnp.int32, (CAP * n_devices, slots), 0)
    if order != tuple(range(n_devices)):
        position = slot % n_devices
        device = jnp.zeros_like(slot)
        for p, d in enumerate(order):
            device = jnp.where(position == p, d, device)
        slot = slot - position + device
    spread_row = lax.broadcasted_iota(jnp.int32, (4 * n_chan, n_chan), 0)
    spread_chan = lax.broadcasted_iota(jnp.int32, (4 * n_chan, n_chan), 1)
    parity = spread_row // (2 * n_chan)
    spread = ((spread_row - parity * 2 * n_chan) == spread_chan * 2 + parity).astype(jnp.bfloat16)
    index_load.wait()
    features_load.wait()
    lengths_load.wait()
    tiles_load.wait()
    owner = index_ref[pl.ds(0, 1), :]
    across = jnp.broadcast_to(owner, (slots, slots))
    down = jnp.sum(jnp.where(here == there, across, 0), axis=1, keepdims=True)
    rank = jnp.sum(jnp.where((down == across) & (here < there), 1, 0), axis=0, keepdims=True)
    target = rank * n_devices + owner
    place = slot == target
    code = jnp.where(place, (index_ref[pl.ds(1, 1), :] + 1).astype(jnp.float32), 0.0)
    code = jnp.broadcast_to(jnp.sum(code, axis=1, keepdims=True), (CAP * n_devices, LANES))
    for c in range(CAP):
        wide[pl.ds(base + CAP * tile_rows + c, n_devices, stride=rows), :] = code[
            c * n_devices : (c + 1) * n_devices
        ]
    place = place.astype(jnp.bfloat16)
    placed = dot(place, tiles_ref[...])
    for q in range(tile_rows):
        for c in range(CAP):
            wide[pl.ds(base + c * tile_rows + q, n_devices, stride=rows), :] = placed[
                c * n_devices : (c + 1) * n_devices, q * LANES : (q + 1) * LANES
            ]
    height = lines * depth
    normed_ref[...] = standardize(features_ref[pl.ds(0, height), :].astype(jnp.float32))
    second = features_ref[pl.ds(height, n_chan), :]
    first = dot(spread, features_ref[pl.ds(height + n_chan, n_chan), :]).astype(jnp.bfloat16)
    groups = n_chan // right_rows
    for t in range(lines):
        normed = normed_ref[pl.ds(t, depth, stride=lines), :].astype(jnp.bfloat16)
        right = dot_nt(second, normed)
        right = jnp.concatenate(
            [right[b * right_rows : (b + 1) * right_rows] for b in range(groups)], axis=1
        )
        for d in range(n_devices):
            wide[pl.ds(d * rows + t * right_rows, right_rows), :] = right
        for parity in range(2):
            left = dot_nt(normed, first[parity * 2 * n_chan : (parity + 1) * 2 * n_chan])
            left = left.astype(jnp.bfloat16).astype(jnp.float32) * (1.0 / depth)
            left_ref[pl.ds((parity * lines + t) * depth, depth), :] = left.astype(jnp.bfloat16)
    low = jnp.zeros_like(column)
    high = jnp.zeros_like(column)
    for i in range(lines):
        token = lax.axis_index("row") * lines + i
        end, below, above = jnp.int32(0), jnp.int32(0), jnp.int32(2**31 - 1)
        for c in range(lengths_ref.shape[0]):
            end = end + lengths_ref[c]
            below = jnp.where(end <= token, jnp.maximum(below, end), below)
            above = jnp.where(end <= token, above, jnp.minimum(above, end))
        low = jnp.where(line == i, below, low)
        high = jnp.where(line == i, above, high)
    same_ref[...] = ((column >= low) & (column < high)).astype(jnp.float32)
    send_ref[...] = wide[...].astype(jnp.bfloat16)
    offset_load.wait()
    weights_load.wait()
    tensor_load.wait()


def pair_kernel(
    n_devices,
    rows,
    tc,
    got_ref,
    left_ref,
    same_ref,
    tensor_ref,
    offset_ref,
    weights_ref,
    out_ref,
    folded,
    wide,
    sums,
    pair,
):
    pair_chan = weights_ref.shape[1]
    n_temp = weights_ref.shape[0] - 2 * pair_chan
    structural = weights_ref[pl.ds(0, n_temp), :]
    sigmoid = weights_ref[pl.ds(n_temp, pair_chan), :]
    content = weights_ref[pl.ds(n_temp + pair_chan, pair_chan), :]
    lines = folded.shape[0]
    right_rows = folded.shape[1] // LANES
    depth = left_ref.shape[0] // (2 * lines)
    n_tokens = n_devices * lines
    n_tiles = n_tokens // tc
    tile_rows = same_ref.shape[0] // n_tiles
    base = lines * right_rows

    width = left_ref.shape[1]
    chans = tensor_ref.shape[0] // width
    half = right_rows // 2
    for p0 in range(half):
        for p in range(p0, chans, 2 * half):
            both = jnp.concatenate(
                [tensor_ref[pl.ds(p * width, width), :], tensor_ref[pl.ds((p + half) * width, width), :]], axis=1
            )
            part = dot(left_ref[...], both).astype(jnp.bfloat16)
            for n in range(2):
                for parity in range(2):
                    d = 2 * (p + n * half) + parity
                    at = (d % right_rows) * LANES + (d // right_rows) * depth
                    for t in range(lines):
                        first = (parity * lines + t) * depth
                        folded[t, pl.ds(at, depth), :] = part[
                            first : first + depth, n * pair_chan : (n + 1) * pair_chan
                        ]

    wide[...] = got_ref[...].astype(jnp.float32)
    few = min(n_devices, 16)
    slots = few * CAP
    span = slots * tile_rows
    kept = n_tiles * tile_rows
    slot_of = lax.broadcasted_iota(jnp.int32, (slots, span), 1) // tile_rows
    slot_is = lax.broadcasted_iota(jnp.int32, (slots, span), 0) == slot_of
    row_of = lax.broadcasted_iota(jnp.int32, (kept, span), 1) % tile_rows
    row = lax.broadcasted_iota(jnp.int32, (kept, span), 0)
    row_is = row % tile_rows == row_of
    wanted = (row // tile_rows + 1).astype(jnp.float32)

    def add_sources(first):
        codes = jnp.concatenate(
            [wide[pl.ds(first * rows + base + CAP * tile_rows + c, few, stride=rows), :] for c in range(CAP)], axis=0
        )
        across = jnp.concatenate([codes] * (span // LANES), axis=1)
        across = jnp.sum(jnp.where(slot_is, across, 0.0), axis=0, keepdims=True)
        landing = jnp.where(row_is & (across == wanted), 1.0, 0.0).astype(jnp.bfloat16)
        tiles = [
            wide[pl.ds((first + q) * rows + base + c * tile_rows, tile_rows), :].astype(jnp.bfloat16)
            for c in range(CAP)
            for q in range(few)
        ]
        counts = [
            jnp.sum(jnp.where(codes == k + 1.0, 1.0, 0.0), axis=0, keepdims=True) for k in range(n_tiles)
        ]
        return dot(landing, jnp.concatenate(tiles, axis=0)), counts

    total, counts = add_sources(0)
    if few < n_devices:
        sums[...] = total

        def add_more(n, counts):
            total, more = add_sources(n * few)
            sums[...] = sums[...] + total
            return tuple(a + b for a, b in zip(counts, more))

        counts = lax.fori_loop(1, n_devices // few, add_more, tuple(counts))
        total = sums[...]
    lhs = jnp.concatenate(
        [
            jnp.concatenate(
                [wide[pl.ds(t * right_rows + g, n_devices, stride=rows), :] for t in range(lines)], axis=0
            ).astype(jnp.bfloat16)
            for g in range(right_rows)
        ],
        axis=1,
    )
    order = exchange_order(n_devices)
    token = lax.broadcasted_iota(jnp.int32, (n_tokens, n_tokens), 0)
    held = lax.broadcasted_iota(jnp.int32, (n_tokens, n_tokens), 1)
    position = held % n_devices
    device = position
    if order != tuple(range(n_devices)):
        device = jnp.zeros_like(held)
        for p, d in enumerate(order):
            device = jnp.where(position == p, d, device)
    swap = (token == device * lines + held // n_devices).astype(jnp.bfloat16)
    lhs = dot(swap, lhs).astype(jnp.bfloat16)
    outer = None
    step = folded.shape[1] // 2
    for at in range(0, folded.shape[1], step):
        term = dot(
            lhs[:, at : at + step],
            jnp.concatenate([folded[i, pl.ds(at, step), :] for i in range(lines)], axis=1),
        )
        outer = term if outer is None else outer + term
    packed = LANES // n_temp
    per_row = tile_rows // lines
    for k in range(n_tiles):
        at = pl.ds(k * tile_rows, tile_rows)
        mean = total[k * tile_rows : (k + 1) * tile_rows] / jnp.maximum(counts[k], 1.0)
        template = (mean * same_ref[at, :]).astype(jnp.bfloat16)
        for h in range(packed):
            part = dot(template[:, h * n_temp : (h + 1) * n_temp], structural)
            for i in range(lines):
                first = i * n_tokens + k * tc + h
                pair[pl.ds(first, per_row, stride=packed), :] = part[i * per_row : (i + 1) * per_row]
    for i in range(lines):
        at = pl.ds(i * n_tokens, n_tokens)
        total = pair[at, :] + (
            outer[:, i * pair_chan : (i + 1) * pair_chan] + offset_ref[...].astype(jnp.float32)
        )
        pair_normed = standardize(total).astype(jnp.bfloat16)
        gate = jax.nn.sigmoid(dot(pair_normed, sigmoid))
        linear = dot(pair_normed, content)
        out_ref[at, :] = (gate * linear).astype(out_ref.dtype)


def grant(*arrays):
    return pltpu.CompilerParams(
        vmem_limit_bytes=sum(2 * math.prod(shape) * jnp.dtype(kind).itemsize for shape, kind in arrays) + (1 << 20)
    )


def on_device(
    aligned_sequences,
    first_factor_matrix,
    second_factor_matrix,
    tensor_matrix,
    tensor_offset,
    structural_duplex_patches,
    patch_source_index,
    patch_target_index,
    structural_matrix,
    polymer_residue_lengths,
    sigmoid_matrix,
    content_matrix,
):
    n_devices = lax.axis_size("row")
    depth, lines, n_feat = aligned_sequences.shape
    slots, width = structural_duplex_patches.shape
    n_chan = first_factor_matrix.shape[1]
    n_temp, pair_chan = structural_matrix.shape
    tc = width // (lines * n_temp)
    n_tokens = lines * n_devices
    n_tiles = n_tokens // tc
    tile_rows = width // LANES
    right_rows = n_chan * depth // LANES
    rows = lines * right_rows + CAP * tile_rows + CAP
    vmem = pl.BlockSpec(memory_space=VMEM)
    hbm = pl.BlockSpec(memory_space=HBM)
    half = n_chan // 2
    f32, bf16, i32 = jnp.float32, jnp.bfloat16, jnp.int32

    arguments = (
        aligned_sequences.reshape(depth * lines, n_feat),
        second_factor_matrix.T,
        structural_duplex_patches,
        patch_source_index.reshape(1, slots),
        patch_target_index.reshape(1, slots),
        first_factor_matrix.T,
        polymer_residue_lengths,
        tensor_matrix.reshape(n_chan, half, 2, pair_chan),
        tensor_offset.reshape(1, pair_chan),
        structural_matrix,
        sigmoid_matrix,
        content_matrix,
    )
    results = (
        ((n_devices * rows, LANES), bf16),
        ((2 * lines * depth, 2 * n_chan), bf16),
        ((n_tiles * tile_rows, LANES), f32),
        ((half, n_chan, 2, pair_chan), bf16),
        ((1, pair_chan), bf16),
        ((n_temp + 2 * pair_chan, pair_chan), bf16),
    )
    scratch = (
        ((depth * lines + 2 * n_chan, n_feat), bf16),
        ((slots, width), bf16),
        ((2, slots), i32),
    )
    packed_wide = ((n_devices * rows, LANES), f32)
    send, left, same, tensor, offset, weights = pl.pallas_call(
        functools.partial(pack_kernel, n_devices, lines, rows, tc),
        out_shape=[jax.ShapeDtypeStruct(*r) for r in results],
        in_specs=[hbm] * len(arguments),
        out_specs=[vmem] * len(results),
        scratch_shapes=[pltpu.VMEM(*a) for a in scratch]
        + [pltpu.SMEM(polymer_residue_lengths.shape, i32), pltpu.VMEM((depth * lines, n_feat), f32)]
        + [pltpu.VMEM(*packed_wide)]
        + [pltpu.SemaphoreType.DMA((7,))],
        compiler_params=grant(*results, *scratch, packed_wide),
    )(*(pltpu.with_memory_space_constraint(a, HBM) for a in arguments))
    got = lax.all_to_all(
        send.reshape(n_devices, rows // 2, 2, LANES),
        "row",
        split_axis=0,
        concat_axis=0,
        tiled=True,
        axis_index_groups=[exchange_order(n_devices)],
    ).reshape(n_devices * rows, LANES)
    tensor = tensor.reshape(n_chan * n_chan, pair_chan)
    scratch = (
        ((lines, n_chan * depth, pair_chan), bf16),
        packed_wide,
        ((n_tiles * tile_rows, LANES), f32),
        ((lines * n_tokens, pair_chan), f32),
    )
    result = ((lines * n_tokens, pair_chan), bf16)
    out = pl.pallas_call(
        functools.partial(pair_kernel, n_devices, rows, tc),
        out_shape=jax.ShapeDtypeStruct(*result),
        in_specs=[vmem] * 6,
        out_specs=vmem,
        scratch_shapes=[pltpu.VMEM(*a) for a in scratch],
        compiler_params=grant(*results, *scratch, result),
    )(got, left, same, tensor, offset, weights)
    return out.reshape(lines, n_tokens, pair_chan)


def solution(mesh):
    placed = (
        P(None, ("grp", "row"), None),
        P(),
        P(),
        P(),
        P(),
        P(("grp", "row"), None),
        P(("grp", "row"), None),
        P(("grp", "row")),
        P(),
        P("grp"),
        P(),
        P(),
    )
    return jax.shard_map(
        on_device,
        mesh=mesh,
        in_specs=placed,
        out_specs=P(("grp", "row"), None, None),
        check_vma=False,
    )
```

```python
import functools
import math

import jax
import jax.numpy as jnp
from jax import lax
from jax.experimental import pallas as pl
from jax.experimental.pallas import tpu as pltpu
from jax.sharding import PartitionSpec as P

CAP = 2
LANES = 128
ORDERS = {16: (11, 0, 2, 8, 5, 7, 3, 1, 15, 14, 4, 12, 13, 10, 9, 6)}
VMEM = pltpu.MemorySpace.VMEM
HBM = pltpu.MemorySpace.HBM


def dot(a, b):
    return jnp.dot(a, b, preferred_element_type=jnp.float32)


def dot_nt(a, b):
    return lax.dot_general(a, b, (((1,), (1,)), ((), ())), preferred_element_type=jnp.float32)


def exchange_order(n_devices):
    return ORDERS.get(n_devices, tuple(range(n_devices)))


def standardize(x):
    centred = x - jnp.mean(x, axis=-1, keepdims=True)
    variance = jnp.mean(centred * centred, axis=-1, keepdims=True)
    return centred * lax.rsqrt(variance + 1e-05)


def pack_kernel(n_devices, lines, rows, tc, *refs):
    (
        x_hbm,
        second_hbm,
        tiles_hbm,
        owner_hbm,
        column_hbm,
        first_hbm,
        lengths_hbm,
        tensor_hbm,
        offset_hbm,
        structural_hbm,
        sigmoid_hbm,
        content_hbm,
        send_ref,
        left_ref,
        same_ref,
        tensor_ref,
        offset_ref,
        weights_ref,
        features_ref,
        tiles_ref,
        index_ref,
        lengths_ref,
        normed_ref,
        wide,
        arrived,
    ) = refs

    def load(n, target, *sources):
        at = 0
        for source in sources:
            size = source.shape[0]
            pltpu.make_async_copy(source, target.at[pl.ds(at, size)], arrived.at[n]).start()
            at = at + size
        return pltpu.make_async_copy(target, target, arrived.at[n])

    index_load = load(0, index_ref, owner_hbm, column_hbm)
    features_load = load(1, features_ref, x_hbm, second_hbm, first_hbm)
    tiles_load = load(2, tiles_ref, tiles_hbm)
    lengths_load = pltpu.make_async_copy(lengths_hbm, lengths_ref, arrived.at[3])
    lengths_load.start()
    offset_load = load(4, offset_ref, offset_hbm)
    weights_load = load(5, weights_ref, structural_hbm, sigmoid_hbm, content_hbm)
    for p in range(tensor_ref.shape[0]):
        pltpu.make_async_copy(tensor_hbm.at[:, p], tensor_ref.at[p], arrived.at[6]).start()
    tensor_load = pltpu.make_async_copy(tensor_ref, tensor_ref, arrived.at[6])
    slots, width = tiles_ref.shape
    depth = left_ref.shape[0] // (2 * lines)
    tile_rows = width // LANES
    n_chan = second_hbm.shape[0]
    right_rows = n_chan * depth // LANES
    base = lines * right_rows
    per_row = tile_rows // lines
    packed = tc // per_row
    row = lax.broadcasted_iota(jnp.int32, same_ref.shape, 0)
    lane = lax.broadcasted_iota(jnp.int32, same_ref.shape, 1)
    column = (row // tile_rows) * tc + (row % per_row) * packed + lane // (LANES // packed)
    line = (row % tile_rows) // per_row
    here = lax.broadcasted_iota(jnp.int32, (slots, slots), 0)
    there = lax.broadcasted_iota(jnp.int32, (slots, slots), 1)
    order = exchange_order(n_devices)
    slot = lax.broadcasted_iota(jnp.int32, (CAP * n_devices, slots), 0)
    if order != tuple(range(n_devices)):
        position = slot % n_devices
        device = jnp.zeros_like(slot)
        for p, d in enumerate(order):
            device = jnp.where(position == p, d, device)
        slot = slot - position + device
    spread_row = lax.broadcasted_iota(jnp.int32, (4 * n_chan, n_chan), 0)
    spread_chan = lax.broadcasted_iota(jnp.int32, (4 * n_chan, n_chan), 1)
    parity = spread_row // (2 * n_chan)
    spread = ((spread_row - parity * 2 * n_chan) == spread_chan * 2 + parity).astype(jnp.bfloat16)
    index_load.wait()
    features_load.wait()
    lengths_load.wait()
    tiles_load.wait()
    owner = index_ref[pl.ds(0, 1), :]
    across = jnp.broadcast_to(owner, (slots, slots))
    down = jnp.sum(jnp.where(here == there, across, 0), axis=1, keepdims=True)
    rank = jnp.sum(jnp.where((down == across) & (here < there), 1, 0), axis=0, keepdims=True)
    target = rank * n_devices + owner
    place = slot == target
    code = jnp.where(place, (index_ref[pl.ds(1, 1), :] + 1).astype(jnp.float32), 0.0)
    code = jnp.broadcast_to(jnp.sum(code, axis=1, keepdims=True), (CAP * n_devices, LANES))
    for c in range(CAP):
        wide[pl.ds(base + CAP * tile_rows + c, n_devices, stride=rows), :] = code[
            c * n_devices : (c + 1) * n_devices
        ]
    height = lines * depth
    normed_ref[...] = standardize(features_ref[pl.ds(0, height), :].astype(jnp.float32))
    second = features_ref[pl.ds(height, n_chan), :]
    first = dot(spread, features_ref[pl.ds(height + n_chan, n_chan), :]).astype(jnp.bfloat16)
    groups = n_chan // right_rows
    for t in range(lines):
        normed = normed_ref[pl.ds(t, depth, stride=lines), :].astype(jnp.bfloat16)
        right = dot_nt(second, normed)
        right = jnp.concatenate(
            [right[b * right_rows : (b + 1) * right_rows] for b in range(groups)], axis=1
        )
        for d in range(n_devices):
            wide[pl.ds(d * rows + t * right_rows, right_rows), :] = right
        for parity in range(2):
            left = dot_nt(normed, first[parity * 2 * n_chan : (parity + 1) * 2 * n_chan])
            left = left.astype(jnp.bfloat16).astype(jnp.float32) * (1.0 / depth)
            left_ref[pl.ds((parity * lines + t) * depth, depth), :] = left.astype(jnp.bfloat16)
    place = place.astype(jnp.bfloat16)
    for q in range(tile_rows):
        placed = dot(place, tiles_ref[:, q * LANES : (q + 1) * LANES])
        for c in range(CAP):
            wide[pl.ds(base + c * tile_rows + q, n_devices, stride=rows), :] = placed[
                c * n_devices : (c + 1) * n_devices
            ]
    low = jnp.zeros_like(column)
    high = jnp.zeros_like(column)
    for i in range(lines):
        token = lax.axis_index("row") * lines + i
        end, below, above = jnp.int32(0), jnp.int32(0), jnp.int32(2**31 - 1)
        for c in range(lengths_ref.shape[0]):
            end = end + lengths_ref[c]
            below = jnp.where(end <= token, jnp.maximum(below, end), below)
            above = jnp.where(end <= token, above, jnp.minimum(above, end))
        low = jnp.where(line == i, below, low)
        high = jnp.where(line == i, above, high)
    same_ref[...] = ((column >= low) & (column < high)).astype(jnp.float32)
    send_ref[...] = wide[...].astype(jnp.bfloat16)
    offset_load.wait()
    weights_load.wait()
    tensor_load.wait()


def pair_kernel(
    n_devices,
    rows,
    tc,
    got_ref,
    left_ref,
    same_ref,
    tensor_ref,
    offset_ref,
    weights_ref,
    out_ref,
    folded,
    wide,
    sums,
    pair,
):
    pair_chan = weights_ref.shape[1]
    n_temp = weights_ref.shape[0] - 2 * pair_chan
    structural = weights_ref[pl.ds(0, n_temp), :]
    sigmoid = weights_ref[pl.ds(n_temp, pair_chan), :]
    content = weights_ref[pl.ds(n_temp + pair_chan, pair_chan), :]
    lines = folded.shape[0]
    right_rows = folded.shape[1] // LANES
    depth = left_ref.shape[0] // (2 * lines)
    n_tokens = n_devices * lines
    n_tiles = n_tokens // tc
    tile_rows = same_ref.shape[0] // n_tiles
    base = lines * right_rows

    width = left_ref.shape[1]
    chans = tensor_ref.shape[0] // width
    half = right_rows // 2
    for p0 in range(half):
        for p in range(p0, chans, 2 * half):
            both = jnp.concatenate(
                [tensor_ref[pl.ds(p * width, width), :], tensor_ref[pl.ds((p + half) * width, width), :]], axis=1
            )
            part = dot(left_ref[...], both).astype(jnp.bfloat16)
            for n in range(2):
                for parity in range(2):
                    d = 2 * (p + n * half) + parity
                    at = (d % right_rows) * LANES + (d // right_rows) * depth
                    for t in range(lines):
                        first = (parity * lines + t) * depth
                        folded[t, pl.ds(at, depth), :] = part[
                            first : first + depth, n * pair_chan : (n + 1) * pair_chan
                        ]

    wide[...] = got_ref[...].astype(jnp.float32)
    few = min(n_devices, 16)
    slots = few * CAP
    span = slots * tile_rows
    kept = n_tiles * tile_rows
    slot_of = lax.broadcasted_iota(jnp.int32, (slots, span), 1) // tile_rows
    slot_is = lax.broadcasted_iota(jnp.int32, (slots, span), 0) == slot_of
    row_of = lax.broadcasted_iota(jnp.int32, (kept, span), 1) % tile_rows
    row = lax.broadcasted_iota(jnp.int32, (kept, span), 0)
    row_is = row % tile_rows == row_of
    wanted = (row // tile_rows + 1).astype(jnp.float32)

    def add_sources(first):
        codes = jnp.concatenate(
            [wide[pl.ds(first * rows + base + CAP * tile_rows + c, few, stride=rows), :] for c in range(CAP)], axis=0
        )
        across = jnp.concatenate([codes] * (span // LANES), axis=1)
        across = jnp.sum(jnp.where(slot_is, across, 0.0), axis=0, keepdims=True)
        landing = jnp.where(row_is & (across == wanted), 1.0, 0.0).astype(jnp.bfloat16)
        tiles = [
            wide[pl.ds((first + q) * rows + base + c * tile_rows, tile_rows), :].astype(jnp.bfloat16)
            for c in range(CAP)
            for q in range(few)
        ]
        counts = [
            jnp.sum(jnp.where(codes == k + 1.0, 1.0, 0.0), axis=0, keepdims=True) for k in range(n_tiles)
        ]
        return dot(landing, jnp.concatenate(tiles, axis=0)), counts

    total, counts = add_sources(0)
    if few < n_devices:
        sums[...] = total

        def add_more(n, counts):
            total, more = add_sources(n * few)
            sums[...] = sums[...] + total
            return tuple(a + b for a, b in zip(counts, more))

        counts = lax.fori_loop(1, n_devices // few, add_more, tuple(counts))
        total = sums[...]
    lhs = jnp.concatenate(
        [
            jnp.concatenate(
                [wide[pl.ds(t * right_rows + g, n_devices, stride=rows), :] for t in range(lines)], axis=0
            ).astype(jnp.bfloat16)
            for g in range(right_rows)
        ],
        axis=1,
    )
    order = exchange_order(n_devices)
    token = lax.broadcasted_iota(jnp.int32, (n_tokens, n_tokens), 0)
    held = lax.broadcasted_iota(jnp.int32, (n_tokens, n_tokens), 1)
    position = held % n_devices
    device = position
    if order != tuple(range(n_devices)):
        device = jnp.zeros_like(held)
        for p, d in enumerate(order):
            device = jnp.where(position == p, d, device)
    swap = (token == device * lines + held // n_devices).astype(jnp.bfloat16)
    lhs = dot(swap, lhs).astype(jnp.bfloat16)
    outer = None
    step = folded.shape[1] // 2
    for at in range(0, folded.shape[1], step):
        term = dot(
            lhs[:, at : at + step],
            jnp.concatenate([folded[i, pl.ds(at, step), :] for i in range(lines)], axis=1),
        )
        outer = term if outer is None else outer + term
    packed = LANES // n_temp
    per_row = tile_rows // lines
    for k in range(n_tiles):
        at = pl.ds(k * tile_rows, tile_rows)
        mean = total[k * tile_rows : (k + 1) * tile_rows] / jnp.maximum(counts[k], 1.0)
        template = (mean * same_ref[at, :]).astype(jnp.bfloat16)
        for h in range(packed):
            part = dot(template[:, h * n_temp : (h + 1) * n_temp], structural)
            for i in range(lines):
                first = i * n_tokens + k * tc + h
                pair[pl.ds(first, per_row, stride=packed), :] = part[i * per_row : (i + 1) * per_row]
    for i in range(lines):
        at = pl.ds(i * n_tokens, n_tokens)
        total = pair[at, :] + (
            outer[:, i * pair_chan : (i + 1) * pair_chan] + offset_ref[...].astype(jnp.float32)
        )
        pair_normed = standardize(total).astype(jnp.bfloat16)
        gate = jax.nn.sigmoid(dot(pair_normed, sigmoid))
        linear = dot(pair_normed, content)
        out_ref[at, :] = (gate * linear).astype(out_ref.dtype)


def grant(*arrays):
    return pltpu.CompilerParams(
        vmem_limit_bytes=sum(2 * math.prod(shape) * jnp.dtype(kind).itemsize for shape, kind in arrays) + (1 << 20)
    )


def on_device(
    aligned_sequences,
    first_factor_matrix,
    second_factor_matrix,
    tensor_matrix,
    tensor_offset,
    structural_duplex_patches,
    patch_source_index,
    patch_target_index,
    structural_matrix,
    polymer_residue_lengths,
    sigmoid_matrix,
    content_matrix,
):
    n_devices = lax.axis_size("row")
    depth, lines, n_feat = aligned_sequences.shape
    slots, width = structural_duplex_patches.shape
    n_chan = first_factor_matrix.shape[1]
    n_temp, pair_chan = structural_matrix.shape
    tc = width // (lines * n_temp)
    n_tokens = lines * n_devices
    n_tiles = n_tokens // tc
    tile_rows = width // LANES
    right_rows = n_chan * depth // LANES
    rows = lines * right_rows + CAP * tile_rows + CAP
    vmem = pl.BlockSpec(memory_space=VMEM)
    hbm = pl.BlockSpec(memory_space=HBM)
    half = n_chan // 2
    f32, bf16, i32 = jnp.float32, jnp.bfloat16, jnp.int32

    arguments = (
        aligned_sequences.reshape(depth * lines, n_feat),
        second_factor_matrix.T,
        structural_duplex_patches,
        patch_source_index.reshape(1, slots),
        patch_target_index.reshape(1, slots),
        first_factor_matrix.T,
        polymer_residue_lengths,
        tensor_matrix.reshape(n_chan, half, 2, pair_chan),
        tensor_offset.reshape(1, pair_chan),
        structural_matrix,
        sigmoid_matrix,
        content_matrix,
    )
    results = (
        ((n_devices * rows, LANES), bf16),
        ((2 * lines * depth, 2 * n_chan), bf16),
        ((n_tiles * tile_rows, LANES), f32),
        ((half, n_chan, 2, pair_chan), bf16),
        ((1, pair_chan), bf16),
        ((n_temp + 2 * pair_chan, pair_chan), bf16),
    )
    scratch = (
        ((depth * lines + 2 * n_chan, n_feat), bf16),
        ((slots, width), bf16),
        ((2, slots), i32),
    )
    packed_wide = ((n_devices * rows, LANES), f32)
    send, left, same, tensor, offset, weights = pl.pallas_call(
        functools.partial(pack_kernel, n_devices, lines, rows, tc),
        out_shape=[jax.ShapeDtypeStruct(*r) for r in results],
        in_specs=[hbm] * len(arguments),
        out_specs=[vmem] * len(results),
        scratch_shapes=[pltpu.VMEM(*a) for a in scratch]
        + [pltpu.SMEM(polymer_residue_lengths.shape, i32), pltpu.VMEM((depth * lines, n_feat), f32)]
        + [pltpu.VMEM(*packed_wide)]
        + [pltpu.SemaphoreType.DMA((7,))],
        compiler_params=grant(*results, *scratch, packed_wide),
    )(*(pltpu.with_memory_space_constraint(a, HBM) for a in arguments))
    got = lax.all_to_all(
        send.reshape(n_devices, rows // 2, 2, LANES),
        "row",
        split_axis=0,
        concat_axis=0,
        tiled=True,
        axis_index_groups=[exchange_order(n_devices)],
    ).reshape(n_devices * rows, LANES)
    tensor = tensor.reshape(n_chan * n_chan, pair_chan)
    scratch = (
        ((lines, n_chan * depth, pair_chan), bf16),
        packed_wide,
        ((n_tiles * tile_rows, LANES), f32),
        ((lines * n_tokens, pair_chan), f32),
    )
    result = ((lines * n_tokens, pair_chan), bf16)
    out = pl.pallas_call(
        functools.partial(pair_kernel, n_devices, rows, tc),
        out_shape=jax.ShapeDtypeStruct(*result),
        in_specs=[vmem] * 6,
        out_specs=vmem,
        scratch_shapes=[pltpu.VMEM(*a) for a in scratch],
        compiler_params=grant(*results, *scratch, result),
    )(got, left, same, tensor, offset, weights)
    return out.reshape(lines, n_tokens, pair_chan)


def solution(mesh):
    placed = (
        P(None, ("grp", "row"), None),
        P(),
        P(),
        P(),
        P(),
        P(("grp", "row"), None),
        P(("grp", "row"), None),
        P(("grp", "row")),
        P(),
        P("grp"),
        P(),
        P(),
    )
    return jax.shard_map(
        on_device,
        mesh=mesh,
        in_specs=placed,
        out_specs=P(("grp", "row"), None, None),
        check_vma=False,
    )
```

```python
import functools
import math

import jax
import jax.numpy as jnp
from jax import lax
from jax.experimental import pallas as pl
from jax.experimental.pallas import tpu as pltpu
from jax.sharding import PartitionSpec as P

CAP = 2
LANES = 128
ORDERS = {16: (11, 0, 9, 8, 2, 7, 3, 1, 13, 14, 4, 12, 5, 10, 15, 6)}
VMEM = pltpu.MemorySpace.VMEM
HBM = pltpu.MemorySpace.HBM


def dot(a, b):
    return jnp.dot(a, b, preferred_element_type=jnp.float32)


def dot_nt(a, b):
    return lax.dot_general(a, b, (((1,), (1,)), ((), ())), preferred_element_type=jnp.float32)


def exchange_order(n_devices):
    return ORDERS.get(n_devices, tuple(range(n_devices)))


def standardize(x):
    centred = x - jnp.mean(x, axis=-1, keepdims=True)
    variance = jnp.mean(centred * centred, axis=-1, keepdims=True)
    return centred * lax.rsqrt(variance + 1e-05)


def pack_kernel(n_devices, lines, rows, tc, *refs):
    (
        x_hbm,
        second_hbm,
        tiles_hbm,
        owner_hbm,
        column_hbm,
        first_hbm,
        lengths_hbm,
        tensor_hbm,
        offset_hbm,
        structural_hbm,
        sigmoid_hbm,
        content_hbm,
        send_ref,
        left_ref,
        same_ref,
        tensor_ref,
        offset_ref,
        weights_ref,
        features_ref,
        tiles_ref,
        index_ref,
        lengths_ref,
        normed_ref,
        wide,
        arrived,
    ) = refs

    def load(n, target, *sources):
        at = 0
        for source in sources:
            size = source.shape[0]
            pltpu.make_async_copy(source, target.at[pl.ds(at, size)], arrived.at[n]).start()
            at = at + size
        return pltpu.make_async_copy(target, target, arrived.at[n])

    index_load = load(0, index_ref, owner_hbm, column_hbm)
    features_load = load(1, features_ref, x_hbm, second_hbm, first_hbm)
    tiles_load = load(2, tiles_ref, tiles_hbm)
    lengths_load = pltpu.make_async_copy(lengths_hbm, lengths_ref, arrived.at[3])
    lengths_load.start()
    offset_load = load(4, offset_ref, offset_hbm)
    weights_load = load(5, weights_ref, structural_hbm, sigmoid_hbm, content_hbm)
    for p in range(tensor_ref.shape[0]):
        pltpu.make_async_copy(tensor_hbm.at[:, p], tensor_ref.at[p], arrived.at[6]).start()
    tensor_load = pltpu.make_async_copy(tensor_ref, tensor_ref, arrived.at[6])
    slots, width = tiles_ref.shape
    depth = left_ref.shape[0] // (2 * lines)
    tile_rows = width // LANES
    n_chan = second_hbm.shape[0]
    right_rows = n_chan * depth // LANES
    base = lines * right_rows
    per_row = tile_rows // lines
    packed = tc // per_row
    row = lax.broadcasted_iota(jnp.int32, same_ref.shape, 0)
    lane = lax.broadcasted_iota(jnp.int32, same_ref.shape, 1)
    column = (row // tile_rows) * tc + (row % per_row) * packed + lane // (LANES // packed)
    line = (row % tile_rows) // per_row
    here = lax.broadcasted_iota(jnp.int32, (slots, slots), 0)
    there = lax.broadcasted_iota(jnp.int32, (slots, slots), 1)
    order = exchange_order(n_devices)
    slot = lax.broadcasted_iota(jnp.int32, (CAP * n_devices, slots), 0)
    if order != tuple(range(n_devices)):
        position = slot % n_devices
        device = jnp.zeros_like(slot)
        for p, d in enumerate(order):
            device = jnp.where(position == p, d, device)
        slot = slot - position + device
    spread_row = lax.broadcasted_iota(jnp.int32, (4 * n_chan, n_chan), 0)
    spread_chan = lax.broadcasted_iota(jnp.int32, (4 * n_chan, n_chan), 1)
    parity = spread_row // (2 * n_chan)
    spread = ((spread_row - parity * 2 * n_chan) == spread_chan * 2 + parity).astype(jnp.bfloat16)
    index_load.wait()
    features_load.wait()
    lengths_load.wait()
    tiles_load.wait()
    owner = index_ref[pl.ds(0, 1), :]
    across = jnp.broadcast_to(owner, (slots, slots))
    down = jnp.sum(jnp.where(here == there, across, 0), axis=1, keepdims=True)
    rank = jnp.sum(jnp.where((down == across) & (here < there), 1, 0), axis=0, keepdims=True)
    target = rank * n_devices + owner
    place = slot == target
    code = jnp.where(place, (index_ref[pl.ds(1, 1), :] + 1).astype(jnp.float32), 0.0)
    code = jnp.broadcast_to(jnp.sum(code, axis=1, keepdims=True), (CAP * n_devices, LANES))
    for c in range(CAP):
        wide[pl.ds(base + CAP * tile_rows + c, n_devices, stride=rows), :] = code[
            c * n_devices : (c + 1) * n_devices
        ]
    height = lines * depth
    normed_ref[...] = standardize(features_ref[pl.ds(0, height), :].astype(jnp.float32))
    second = features_ref[pl.ds(height, n_chan), :]
    first = dot(spread, features_ref[pl.ds(height + n_chan, n_chan), :]).astype(jnp.bfloat16)
    groups = n_chan // right_rows
    for t in range(lines):
        normed = normed_ref[pl.ds(t, depth, stride=lines), :].astype(jnp.bfloat16)
        right = dot_nt(second, normed)
        right = jnp.concatenate(
            [right[b * right_rows : (b + 1) * right_rows] for b in range(groups)], axis=1
        )
        for d in range(n_devices):
            wide[pl.ds(d * rows + t * right_rows, right_rows), :] = right
        for parity in range(2):
            left = dot_nt(normed, first[parity * 2 * n_chan : (parity + 1) * 2 * n_chan])
            left = left.astype(jnp.bfloat16).astype(jnp.float32) * (1.0 / depth)
            left_ref[pl.ds((parity * lines + t) * depth, depth), :] = left.astype(jnp.bfloat16)
    place = place.astype(jnp.bfloat16)
    for q in range(tile_rows):
        placed = dot(place, tiles_ref[:, q * LANES : (q + 1) * LANES])
        for c in range(CAP):
            wide[pl.ds(base + c * tile_rows + q, n_devices, stride=rows), :] = placed[
                c * n_devices : (c + 1) * n_devices
            ]
    low = jnp.zeros_like(column)
    high = jnp.zeros_like(column)
    for i in range(lines):
        token = lax.axis_index("row") * lines + i
        end, below, above = jnp.int32(0), jnp.int32(0), jnp.int32(2**31 - 1)
        for c in range(lengths_ref.shape[0]):
            end = end + lengths_ref[c]
            below = jnp.where(end <= token, jnp.maximum(below, end), below)
            above = jnp.where(end <= token, above, jnp.minimum(above, end))
        low = jnp.where(line == i, below, low)
        high = jnp.where(line == i, above, high)
    same_ref[...] = ((column >= low) & (column < high)).astype(jnp.float32)
    send_ref[...] = wide[...].astype(jnp.bfloat16)
    offset_load.wait()
    weights_load.wait()
    tensor_load.wait()


def pair_kernel(
    n_devices,
    rows,
    tc,
    got_ref,
    left_ref,
    same_ref,
    tensor_ref,
    offset_ref,
    weights_ref,
    out_ref,
    folded,
    wide,
    sums,
    pair,
):
    pair_chan = weights_ref.shape[1]
    n_temp = weights_ref.shape[0] - 2 * pair_chan
    structural = weights_ref[pl.ds(0, n_temp), :]
    sigmoid = weights_ref[pl.ds(n_temp, pair_chan), :]
    content = weights_ref[pl.ds(n_temp + pair_chan, pair_chan), :]
    lines = folded.shape[0]
    right_rows = folded.shape[1] // LANES
    depth = left_ref.shape[0] // (2 * lines)
    n_tokens = n_devices * lines
    n_tiles = n_tokens // tc
    tile_rows = same_ref.shape[0] // n_tiles
    base = lines * right_rows

    width = left_ref.shape[1]
    chans = tensor_ref.shape[0] // width
    half = right_rows // 2
    for p0 in range(half):
        for p in range(p0, chans, 2 * half):
            both = jnp.concatenate(
                [tensor_ref[pl.ds(p * width, width), :], tensor_ref[pl.ds((p + half) * width, width), :]], axis=1
            )
            part = dot(left_ref[...], both).astype(jnp.bfloat16)
            for n in range(2):
                for parity in range(2):
                    d = 2 * (p + n * half) + parity
                    at = (d % right_rows) * LANES + (d // right_rows) * depth
                    for t in range(lines):
                        first = (parity * lines + t) * depth
                        folded[t, pl.ds(at, depth), :] = part[
                            first : first + depth, n * pair_chan : (n + 1) * pair_chan
                        ]

    wide[...] = got_ref[...].astype(jnp.float32)
    few = min(n_devices, 16)
    slots = few * CAP
    span = slots * tile_rows
    kept = n_tiles * tile_rows
    slot_of = lax.broadcasted_iota(jnp.int32, (slots, span), 1) // tile_rows
    slot_is = lax.broadcasted_iota(jnp.int32, (slots, span), 0) == slot_of
    row_of = lax.broadcasted_iota(jnp.int32, (kept, span), 1) % tile_rows
    row = lax.broadcasted_iota(jnp.int32, (kept, span), 0)
    row_is = row % tile_rows == row_of
    wanted = (row // tile_rows + 1).astype(jnp.float32)

    def add_sources(first):
        codes = jnp.concatenate(
            [wide[pl.ds(first * rows + base + CAP * tile_rows + c, few, stride=rows), :] for c in range(CAP)], axis=0
        )
        across = jnp.concatenate([codes] * (span // LANES), axis=1)
        across = jnp.sum(jnp.where(slot_is, across, 0.0), axis=0, keepdims=True)
        landing = jnp.where(row_is & (across == wanted), 1.0, 0.0).astype(jnp.bfloat16)
        tiles = [
            wide[pl.ds((first + q) * rows + base + c * tile_rows, tile_rows), :].astype(jnp.bfloat16)
            for c in range(CAP)
            for q in range(few)
        ]
        counts = [
            jnp.sum(jnp.where(codes == k + 1.0, 1.0, 0.0), axis=0, keepdims=True) for k in range(n_tiles)
        ]
        return dot(landing, jnp.concatenate(tiles, axis=0)), counts

    total, counts = add_sources(0)
    if few < n_devices:
        sums[...] = total

        def add_more(n, counts):
            total, more = add_sources(n * few)
            sums[...] = sums[...] + total
            return tuple(a + b for a, b in zip(counts, more))

        counts = lax.fori_loop(1, n_devices // few, add_more, tuple(counts))
        total = sums[...]
    lhs = jnp.concatenate(
        [
            jnp.concatenate(
                [wide[pl.ds(t * right_rows + g, n_devices, stride=rows), :] for t in range(lines)], axis=0
            ).astype(jnp.bfloat16)
            for g in range(right_rows)
        ],
        axis=1,
    )
    order = exchange_order(n_devices)
    token = lax.broadcasted_iota(jnp.int32, (n_tokens, n_tokens), 0)
    held = lax.broadcasted_iota(jnp.int32, (n_tokens, n_tokens), 1)
    position = held % n_devices
    device = position
    if order != tuple(range(n_devices)):
        device = jnp.zeros_like(held)
        for p, d in enumerate(order):
            device = jnp.where(position == p, d, device)
    swap = (token == device * lines + held // n_devices).astype(jnp.bfloat16)
    lhs = dot(swap, lhs).astype(jnp.bfloat16)
    outer = None
    step = folded.shape[1] // 2
    for at in range(0, folded.shape[1], step):
        term = dot(
            lhs[:, at : at + step],
            jnp.concatenate([folded[i, pl.ds(at, step), :] for i in range(lines)], axis=1),
        )
        outer = term if outer is None else outer + term
    packed = LANES // n_temp
    per_row = tile_rows // lines
    for k in range(n_tiles):
        at = pl.ds(k * tile_rows, tile_rows)
        mean = total[k * tile_rows : (k + 1) * tile_rows] / jnp.maximum(counts[k], 1.0)
        template = (mean * same_ref[at, :]).astype(jnp.bfloat16)
        for h in range(packed):
            part = dot(template[:, h * n_temp : (h + 1) * n_temp], structural)
            for i in range(lines):
                first = i * n_tokens + k * tc + h
                pair[pl.ds(first, per_row, stride=packed), :] = part[i * per_row : (i + 1) * per_row]
    for i in range(lines):
        at = pl.ds(i * n_tokens, n_tokens)
        total = pair[at, :] + (
            outer[:, i * pair_chan : (i + 1) * pair_chan] + offset_ref[...].astype(jnp.float32)
        )
        pair_normed = standardize(total).astype(jnp.bfloat16)
        gate = jax.nn.sigmoid(dot(pair_normed, sigmoid))
        linear = dot(pair_normed, content)
        out_ref[at, :] = (gate * linear).astype(out_ref.dtype)


def grant(*arrays):
    return pltpu.CompilerParams(
        vmem_limit_bytes=sum(2 * math.prod(shape) * jnp.dtype(kind).itemsize for shape, kind in arrays) + (1 << 20)
    )


def on_device(
    aligned_sequences,
    first_factor_matrix,
    second_factor_matrix,
    tensor_matrix,
    tensor_offset,
    structural_duplex_patches,
    patch_source_index,
    patch_target_index,
    structural_matrix,
    polymer_residue_lengths,
    sigmoid_matrix,
    content_matrix,
):
    n_devices = lax.axis_size("row")
    depth, lines, n_feat = aligned_sequences.shape
    slots, width = structural_duplex_patches.shape
    n_chan = first_factor_matrix.shape[1]
    n_temp, pair_chan = structural_matrix.shape
    tc = width // (lines * n_temp)
    n_tokens = lines * n_devices
    n_tiles = n_tokens // tc
    tile_rows = width // LANES
    right_rows = n_chan * depth // LANES
    rows = lines * right_rows + CAP * tile_rows + CAP
    vmem = pl.BlockSpec(memory_space=VMEM)
    hbm = pl.BlockSpec(memory_space=HBM)
    half = n_chan // 2
    f32, bf16, i32 = jnp.float32, jnp.bfloat16, jnp.int32

    arguments = (
        aligned_sequences.reshape(depth * lines, n_feat),
        second_factor_matrix.T,
        structural_duplex_patches,
        patch_source_index.reshape(1, slots),
        patch_target_index.reshape(1, slots),
        first_factor_matrix.T,
        polymer_residue_lengths,
        tensor_matrix.reshape(n_chan, half, 2, pair_chan),
        tensor_offset.reshape(1, pair_chan),
        structural_matrix,
        sigmoid_matrix,
        content_matrix,
    )
    results = (
        ((n_devices * rows, LANES), bf16),
        ((2 * lines * depth, 2 * n_chan), bf16),
        ((n_tiles * tile_rows, LANES), f32),
        ((half, n_chan, 2, pair_chan), bf16),
        ((1, pair_chan), bf16),
        ((n_temp + 2 * pair_chan, pair_chan), bf16),
    )
    scratch = (
        ((depth * lines + 2 * n_chan, n_feat), bf16),
        ((slots, width), bf16),
        ((2, slots), i32),
    )
    packed_wide = ((n_devices * rows, LANES), f32)
    send, left, same, tensor, offset, weights = pl.pallas_call(
        functools.partial(pack_kernel, n_devices, lines, rows, tc),
        out_shape=[jax.ShapeDtypeStruct(*r) for r in results],
        in_specs=[hbm] * len(arguments),
        out_specs=[vmem] * len(results),
        scratch_shapes=[pltpu.VMEM(*a) for a in scratch]
        + [pltpu.SMEM(polymer_residue_lengths.shape, i32), pltpu.VMEM((depth * lines, n_feat), f32)]
        + [pltpu.VMEM(*packed_wide)]
        + [pltpu.SemaphoreType.DMA((7,))],
        compiler_params=grant(*results, *scratch, packed_wide),
    )(*(pltpu.with_memory_space_constraint(a, HBM) for a in arguments))
    got = lax.all_to_all(
        send.reshape(n_devices, rows // 2, 2, LANES),
        "row",
        split_axis=0,
        concat_axis=0,
        tiled=True,
        axis_index_groups=[exchange_order(n_devices)],
    ).reshape(n_devices * rows, LANES)
    tensor = tensor.reshape(n_chan * n_chan, pair_chan)
    scratch = (
        ((lines, n_chan * depth, pair_chan), bf16),
        packed_wide,
        ((n_tiles * tile_rows, LANES), f32),
        ((lines * n_tokens, pair_chan), f32),
    )
    result = ((lines * n_tokens, pair_chan), bf16)
    out = pl.pallas_call(
        functools.partial(pair_kernel, n_devices, rows, tc),
        out_shape=jax.ShapeDtypeStruct(*result),
        in_specs=[vmem] * 6,
        out_specs=vmem,
        scratch_shapes=[pltpu.VMEM(*a) for a in scratch],
        compiler_params=grant(*results, *scratch, result),
    )(got, left, same, tensor, offset, weights)
    return out.reshape(lines, n_tokens, pair_chan)


def solution(mesh):
    placed = (
        P(None, ("grp", "row"), None),
        P(),
        P(),
        P(),
        P(),
        P(("grp", "row"), None),
        P(("grp", "row"), None),
        P(("grp", "row")),
        P(),
        P("grp"),
        P(),
        P(),
    )
    return jax.shard_map(
        on_device,
        mesh=mesh,
        in_specs=placed,
        out_specs=P(("grp", "row"), None, None),
        check_vma=False,
    )
```
